32 devices in a mesh: groups: 2 (over y), users: 4 (over z), mp: 2 (over x), helpers: 2 (over core).
Axes of the slice: x: 2, y: 2, z: 4, core: 2. Of those that a mesh axis runs over, the one named last changes fastest.
Arguments:
- candidates: bfloat16 [32, 128, 1024], P(('groups', 'users', 'helpers')), parts along dimension 0, may hold values from -6 to 6
- block_user: int32 [32], P(('groups', 'users', 'helpers')), parts along dimension 0, may hold values from 0 to 31, as said below
- block_count: int32 [32], P(('groups', 'users', 'helpers')), parts along dimension 0, may hold values from 16 to 32, as said below
- own_map: int32 [64], P('groups'), parts along dimension 0, may hold values from 0 to 31, as said below
- history_key_cache: bfloat16 [64, 512, 1024], P(('groups', 'users'), None, 'mp'), parts along dimension 0, may hold values from -6 to 6
- cache_values: bfloat16 [64, 512, 1024], P(('groups', 'users'), None, 'mp'), parts along dimension 0, may hold values from -64 to 64
- w_query_unit: bfloat16 [2, 1024, 1024], P(None, None, 'mp'), may hold values from -0.1875 to 0.1875
- time_bias: float32 [8, 512], P('mp'), may hold values from -5 to 5
- output_weight: bfloat16 [1024, 1024], P('mp'), may hold values from -0.1875 to 0.1875
- w_score: float32 [1024], P('mp'), may hold values from -0.1875 to 0.1875
Outputs:
- scores: float32 [32, 128], P(('groups', 'users', 'helpers')), parts along dimension 0
The draws below stay inside these ranges and needn't reach their ends.
There are 2 independent parts, one for each index of `groups`. The reference program is written for one: setup_inputs(seed, part) draws one part's arguments, and reference() takes and returns one part's arrays. A program takes and returns all parts, laid end to end along the dimension named above; an argument that names none is the same for every part. Nothing has to cross between parts.
Inputs may be any that keep to these rules, and one draw needn't show every extreme that they name: own_map is a permutation of the users; user u's history is row own_map[u] of the caches. `block_user`: the 2 blocks of one device belong to users whose cache rows, divided by 8, are all different; in every draw one such quotient is that of a block on every device. `block_count`: on every device some block has exactly 32 live candidates.
All inputs are finite; a program needn't handle non-finite values.
Results may differ from the reference program's by a relative error of at most 0.003.
Values may be sent and summed in bfloat16 or wider, within the bound.
A program may use at most 128 MiB of HBM per device.

```python
import math
import jax
import jax.numpy as jnp
from jax import lax

D = 1024
H = 8
L = 512
U_DEV = 8
BLOCK = 128
MOST = 32
OWNERS = 4
SOURCES = 8
B_DEV = 2
BLOCKS = 16
USERS = 32


def routing_plan(key):
    anchor = jax.random.fold_in(key, 7)
    owner_perm = jax.random.permutation(jax.random.fold_in(anchor, 1), USERS).astype(jnp.int32)
    hottest = jax.random.randint(jax.random.fold_in(anchor, 2), (), 0, OWNERS).astype(jnp.int32)
    source_keys = jax.random.split(jax.random.fold_in(anchor, 3), SOURCES)

    def one_source(source_key):
        leading_key = jax.random.fold_in(source_key, 1)
        second_key = jax.random.fold_in(source_key, 2)
        third_key = jax.random.fold_in(source_key, 3)
        others = jax.random.permutation(leading_key, OWNERS - 1).astype(jnp.int32)
        others = others + (others >= hottest).astype(jnp.int32)
        targets = jnp.concatenate([hottest[None], others])[:B_DEV]
        row_permuter = jax.random.permutation(second_key, B_DEV)
        targets = targets[row_permuter]
        local_slot = jax.random.randint(third_key, (B_DEV,), 0, U_DEV).astype(jnp.int32)
        return targets * U_DEV + local_slot
    row_ids = jax.vmap(one_source)(source_keys).reshape(-1)
    inverse = jnp.zeros((USERS,), jnp.int32).at[owner_perm].set(jnp.arange(USERS, dtype=jnp.int32))
    user_ids = inverse[row_ids]
    return (owner_perm, user_ids.astype(jnp.int32))


def draw_own_map(key, part):
    return routing_plan(key)[0]


def draw_block_user(key, part):
    return routing_plan(key)[1]


def draw_block_count(key, part):
    counted = jax.random.randint(jax.random.fold_in(key, 11), (SOURCES, B_DEV), MOST // 2, MOST + 1).astype(jnp.int32)
    fullest = jax.random.randint(jax.random.fold_in(key, 12), (SOURCES, 1), 0, B_DEV).astype(jnp.int32)
    column_ids = jnp.arange(B_DEV, dtype=jnp.int32)[None, :]
    counted = jnp.where(column_ids == fullest, MOST, counted)
    return counted.reshape(-1).astype(jnp.int32)


def draw_cache_values(key, part):
    leading_key = jax.random.fold_in(key, 21)
    second_key = jax.random.fold_in(key, 22)
    scales = jnp.exp(jax.random.uniform(leading_key, (USERS, 1, D), jnp.float32, 0.0, math.log(10.0)))
    noise = jnp.clip(jax.random.normal(second_key, (USERS, L, D), jnp.float32), -4.0, 4.0)
    drawn = noise * scales
    return drawn.astype(jnp.bfloat16)


def block_scale(stream_key, dims, shards, smallest, top_value):
    def one(position, parts):
        draws = jax.random.uniform(jax.random.fold_in(jax.random.fold_in(stream_key, 6), position), (parts,), jnp.float32, smallest / len(shards), top_value / len(shards))
        return jnp.repeat(jnp.exp(draws), dims[position] // parts).reshape((-1,) + (1,) * (len(dims) - position - 1))

    level = one(*shards[0])
    for cut in shards[1:]:
        level = level * one(*cut)
    return level


def bell_draw(stream_key, shape, scale, limit, cuts=(), held_as=jnp.bfloat16):
    array = jax.random.normal(stream_key, shape, jnp.float32) * scale
    if len(cuts) > 0:
        array = block_scale(stream_key, shape, cuts, -0.22, 0.18) * array
    return jnp.clip(array, min=-limit, max=limit).astype(held_as)


def setup_inputs(seed: int = 0, part: int = 0) -> dict:
    splits = jax.random.split(jax.random.key(seed), 11)
    own_keys = jax.random.split(jax.random.fold_in(splits[10], part), 11)
    return {
        "candidates": bell_draw(own_keys[0], (BLOCKS, BLOCK, D), 1.0, 6.0, ((0, 8),)),
        "block_user": draw_block_user(jax.random.fold_in(jax.random.fold_in(splits[10], part), 71), part),
        "block_count": draw_block_count(jax.random.fold_in(jax.random.fold_in(splits[10], part), 71), part),
        "own_map": draw_own_map(jax.random.fold_in(jax.random.fold_in(splits[10], part), 71), part),
        "history_key_cache": bell_draw(own_keys[4], (USERS, L, D), 1.0, 6.0, ((0, 4), (2, 2))),
        "cache_values": draw_cache_values(jax.random.fold_in(jax.random.fold_in(splits[10], part), 71), part),
        "w_query_unit": bell_draw(splits[6], (2, D, D), D ** -0.5, 0.1875, ((2, 2),)),
        "time_bias": bell_draw(splits[7], (H, L), 1.0, 5.0, ((0, 2),), jnp.float32),
        "output_weight": bell_draw(splits[8], (D, D), D ** -0.5, 0.1875, ((0, 2),)),
        "w_score": bell_draw(splits[9], (D,), D ** -0.5, 0.1875, ((0, 2),), jnp.float32),
    }


EPSILON = 1e-05

def reference(candidates, block_user, block_count, own_map, history_key_cache, cache_values, w_query_unit, time_bias, output_weight, w_score):
    heads = time_bias.shape[0]
    model_width = candidates.shape[2]
    head_size = model_width // heads
    storage = own_map[block_user].astype(jnp.int32)

    def one_block(block_item):
        block_rows_in, live_count, row_index = block_item
        block_rows_in = block_rows_in[:MOST]
        query_bf = jax.nn.silu(jnp.dot(block_rows_in, w_query_unit[0], preferred_element_type=jnp.float32)).astype(jnp.bfloat16)
        unit_gate = jax.nn.silu(jnp.dot(block_rows_in, w_query_unit[1], preferred_element_type=jnp.float32))
        key_rows = lax.dynamic_index_in_dim(history_key_cache, row_index, 0, keepdims=False)
        value_rows = lax.dynamic_index_in_dim(cache_values, row_index, 0, keepdims=False)
        query_heads = lax.optimization_barrier(query_bf).astype(jnp.float32).reshape(MOST, heads, head_size)
        key_heads = key_rows.astype(jnp.float32).reshape(-1, heads, head_size)
        value_heads = value_rows.astype(jnp.float32).reshape(-1, heads, head_size)
        logits = jnp.einsum('nhd,lhd->hnl', query_heads, key_heads) * head_size ** (-0.5) + time_bias[:, None, :]
        weight_bf = jax.nn.silu(logits).astype(jnp.bfloat16)
        weights = lax.optimization_barrier(weight_bf).astype(jnp.float32)
        mixture = jnp.einsum('hnl,lhd->nhd', weights, value_heads).reshape(MOST, model_width)
        row_mean = lax.optimization_barrier(jnp.mean(mixture, axis=1, keepdims=True))
        spread = lax.optimization_barrier(jnp.mean(mixture * mixture, axis=1, keepdims=True)) - row_mean * row_mean
        normed = (mixture - row_mean) * lax.rsqrt(spread + EPSILON)
        gate_applied_rows = (normed * unit_gate).astype(jnp.bfloat16)
        out_rows = jnp.dot(gate_applied_rows, output_weight, preferred_element_type=jnp.float32)
        block_scores = lax.optimization_barrier(jnp.sum(jax.nn.silu(block_rows_in.astype(jnp.float32) + out_rows) * w_score, axis=1))
        live_mask = jnp.arange(MOST, dtype=jnp.int32) < live_count
        block_scores = jnp.where(live_mask, block_scores, jnp.zeros_like(block_scores))
        return jnp.concatenate([block_scores, jnp.zeros((BLOCK - MOST,), block_scores.dtype)])
    return lax.map(one_block, (candidates, block_count, storage), batch_size=8)
```

```python
import functools

import jax
import jax.numpy as jnp
from jax import lax
from jax.experimental import pallas as pl
from jax.experimental.pallas import tpu as pltpu
from jax.sharding import PartitionSpec as P

EPSILON = 1e-05
MOST = 32
LANES = 128
SUBLANES = 8
MESH = pl.DeviceIdType.MESH
F32 = jnp.float32
BF16 = jnp.bfloat16


def silu(v):
    half = 0.5 * v
    return half + half * jnp.tanh(half)


def kernel(
    sizes,
    user_hbm,
    count_hbm,
    map_hbm,
    cand_ref,
    key_ref,
    value_ref,
    wqu_ref,
    bias_ref,
    wout_ref,
    wsc_ref,
    out_ref,
    user_ref,
    count_ref,
    map_ref,
    x_v,
    wqu_v,
    key_v,
    value_v,
    wout_v,
    bias_v,
    wsc_v,
    q_v,
    q_send,
    q_recv,
    tag_send,
    tag_recv,
    gate_v,
    mix_send,
    mix_recv,
    stat_send,
    stat_recv,
    part_v,
    load_sem,
    tag_ssem,
    tag_rsem,
    q_ssem,
    q_rsem,
    mix_ssem,
    mix_rsem,
    stat_ssem,
    stat_rsem,
    wsc_ssem,
    wsc_rsem,
    part_ssem,
    part_rsem,
):
    owners, parts = sizes
    u = lax.axis_index("users")
    m = lax.axis_index("mp")
    blocks, most, width = x_v.shape
    users_here, length, local = key_v.shape
    heads = bias_v.shape[0]
    head = local // heads
    rows = blocks * most
    tiles = most // SUBLANES

    def remote(src, dst, ssem, rsem, **device):
        return pltpu.make_async_remote_copy(
            src_ref=src,
            dst_ref=dst,
            send_sem=ssem,
            recv_sem=rsem,
            device_id=device,
            device_id_type=MESH,
        )

    def off(index, step, size):
        return lax.rem(index + step, size)

    barrier = pltpu.get_barrier_semaphore()
    for d in range(owners):
        for e in range(parts):
            if d or e:
                pl.semaphore_signal(
                    barrier,
                    inc=1,
                    device_id={"users": off(u, d, owners), "mp": off(m, e, parts)},
                    device_id_type=MESH,
                )

    n = blocks
    scalars = [
        pltpu.make_async_copy(src, dst, load_sem.at[n + 7 + i])
        for i, (src, dst) in enumerate(
            ((user_hbm, user_ref), (map_hbm, map_ref), (count_hbm, count_ref))
        )
    ]
    loads = [pltpu.make_async_copy(cand_ref.at[b, pl.ds(0, most)], x_v.at[b], load_sem.at[b]) for b in range(blocks)]
    load_q = pltpu.make_async_copy(wqu_ref.at[0], wqu_v.at[0], load_sem.at[n])
    load_g = pltpu.make_async_copy(wqu_ref.at[1], wqu_v.at[1], load_sem.at[n + 1])
    load_k = pltpu.make_async_copy(key_ref, key_v, load_sem.at[n + 2])
    load_v = pltpu.make_async_copy(value_ref, value_v, load_sem.at[n + 3])
    load_w = pltpu.make_async_copy(wout_ref, wout_v, load_sem.at[n + 4])
    load_b = pltpu.make_async_copy(bias_ref, bias_v, load_sem.at[n + 5])
    load_s = pltpu.make_async_copy(wsc_ref, wsc_v.at[m], load_sem.at[n + 6])
    for load in scalars + loads + [load_q]:
        load.start()
    for load in scalars:
        load.wait()

    place = [map_ref[user_ref[b]] for b in range(blocks)]
    owner = [p // users_here for p in place]
    row = [p - o * users_here for p, o in zip(place, owner)]

    def routed(o):
        block, line = jnp.int32(0), jnp.int32(0)
        for b in range(blocks):
            hit = owner[b] == o
            block = jnp.where(hit, b, block)
            line = jnp.where(hit, row[b], line)
        return block, line

    targets = [off(u, d, owners) for d in range(owners)]
    routes = [routed(o) for o in targets]
    for o, (block, line) in zip(targets, routes):
        tag_send[o] = jnp.full(tag_send.shape[1:], line, jnp.int32)

    for load in loads:
        load.wait()
    load_q.wait()
    for load in (load_k, load_b, load_v, load_g, load_s, load_w):
        load.start()
    x = x_v[...].reshape(rows, width)
    query = silu(jnp.dot(x, wqu_v[0], preferred_element_type=F32)).astype(BF16)
    q_v[...] = query.reshape(blocks, most, local)
    for d in range(1, owners):
        q_send[targets[d]] = q_v[routes[d][0]]

    pl.semaphore_wait(barrier, owners * parts - 1)

    sends = []

    def start(copy):
        copy.start()
        sends.append(copy)

    for d in range(1, owners):
        o = targets[d]
        start(remote(tag_send.at[o], tag_recv.at[u], tag_ssem.at[o], tag_rsem.at[u], users=o))
        start(remote(q_send.at[o], q_recv.at[u], q_ssem.at[o], q_rsem.at[u], users=o))
    load_s.wait()
    for d in range(1, parts):
        p = off(m, d, parts)
        start(remote(wsc_v.at[m], wsc_v.at[m], wsc_ssem.at[p], wsc_rsem.at[m], mp=p))

    load_b.wait()
    load_k.wait()
    load_v.wait()
    scale = head ** (-0.5)
    lane = lax.broadcasted_iota(jnp.int32, (SUBLANES, LANES), 1)

    def attend(query_of, line):
        found = []
        for h in range(heads):
            cols = pl.ds(h * head, head)
            keys = key_v[line, :, cols]
            values = value_v[line, :, cols]
            logits = lax.dot_general(
                query_of(cols), keys, (((1,), (1,)), ((), ())), preferred_element_type=F32
            )
            weights = silu(logits * scale + bias_v[pl.ds(h, 1), :]).astype(BF16)
            found.append(jnp.dot(weights, values, preferred_element_type=F32))
        total = sum(jnp.sum(f, axis=1, keepdims=True) for f in found)
        mean = total / local
        centred = [f - mean for f in found]
        square = sum(jnp.sum(f * f, axis=1, keepdims=True) for f in centred)
        stat = jnp.zeros((SUBLANES, LANES), F32)
        for t in range(tiles):
            part = slice(t * SUBLANES, (t + 1) * SUBLANES)
            stat = jnp.where(lane == t, mean[part], stat)
            stat = jnp.where(lane == tiles + t, square[part], stat)
        return [f.astype(BF16) for f in centred], stat

    def put(ref, index, pieces):
        for h in range(heads):
            ref[index, :, pl.ds(h * head, head)] = pieces[h]

    own_block, own_line = routes[0]
    pieces, stat = attend(lambda cols: q_v[own_block, :, cols], own_line)
    put(mix_recv, u, pieces)
    stat_recv[m, u] = stat
    for d in range(1, parts):
        p = off(m, d, parts)
        start(remote(stat_recv.at[m, u], stat_recv.at[m, u], stat_ssem.at[p, u], stat_rsem.at[m, u], mp=p))

    load_g.wait()
    gate_v[...] = silu(jnp.dot(x, wqu_v[1], preferred_element_type=F32))

    for d in range(1, owners):
        s = off(u, owners - d, owners)
        remote(tag_send.at[s], tag_recv.at[s], tag_ssem.at[s], tag_rsem.at[s], users=s).wait_recv()
        remote(q_send.at[s], q_recv.at[s], q_ssem.at[s], q_rsem.at[s], users=s).wait_recv()
        line = tag_recv[s, 0, 0]
        pieces, stat = attend(lambda cols: q_recv[s, :, cols], line)
        put(mix_send, s, pieces)
        stat_send[s] = stat
        start(remote(mix_send.at[s], mix_recv.at[u], mix_ssem.at[s], mix_rsem.at[u], users=s))
        for e in range(parts):
            p = off(m, e, parts)
            start(remote(stat_send.at[s], stat_recv.at[m, u], stat_ssem.at[p, s], stat_rsem.at[m, u], users=s, mp=p))

    load_w.wait()
    for d in range(1, parts):
        p = off(m, d, parts)
        remote(wsc_v.at[p], wsc_v.at[p], wsc_ssem.at[p], wsc_rsem.at[p], mp=p).wait_recv()
    for d in range(owners):
        s = targets[d]
        for e in range(parts):
            if d or e:
                p = off(m, e, parts)
                remote(
                    stat_send.at[s], stat_recv.at[p, s], stat_ssem.at[p, s], stat_rsem.at[p, s], users=s, mp=p
                ).wait_recv()
        if d:
            remote(mix_send.at[s], mix_recv.at[s], mix_ssem.at[s], mix_rsem.at[s], users=s).wait_recv()

    gated = []
    for b in range(blocks):
        mine = mix_recv[owner[b]].astype(F32)
        means, squares = [], []
        for p in range(parts):
            stat = stat_recv[p, owner[b]]
            means.append(jnp.concatenate([stat[:, t : t + 1] for t in range(tiles)], axis=0))
            squares.append(jnp.concatenate([stat[:, tiles + t : tiles + t + 1] for t in range(tiles)], axis=0))
        row_mean = sum(means) / parts
        spread = sum(squares) / (parts * local) + sum((a - row_mean) * (a - row_mean) for a in means) / parts
        factor = lax.rsqrt(spread + EPSILON)
        stat = stat_recv[m, owner[b]]
        mean = jnp.concatenate([stat[:, t : t + 1] for t in range(tiles)], axis=0)
        gate = gate_v[pl.ds(b * most, most), :]
        gated.append(((mine + (mean - row_mean)) * factor * gate).astype(BF16))
    gated = jnp.concatenate(gated, axis=0)
    part_v[m] = jnp.dot(gated, wout_v[...], preferred_element_type=F32).astype(BF16)
    for d in range(1, parts):
        p = off(m, d, parts)
        start(remote(part_v.at[m], part_v.at[m], part_ssem.at[p], part_rsem.at[m], mp=p))
    for d in range(1, parts):
        p = off(m, d, parts)
        remote(part_v.at[p], part_v.at[p], part_ssem.at[p], part_rsem.at[p], mp=p).wait_recv()
    out_rows = part_v[0].astype(F32)
    for p in range(1, parts):
        out_rows = out_rows + part_v[p].astype(F32)
    shown = silu(x_v[...].reshape(rows, width).astype(F32) + out_rows)
    folded = jnp.zeros((rows, LANES), F32)
    for p in range(parts):
        for k in range(local // LANES):
            term = shown[:, p * local + k * LANES : p * local + (k + 1) * LANES]
            folded = folded + term * wsc_v[p, :, pl.ds(k * LANES, LANES)]
    block_rows = out_ref.shape[1]
    spot = lax.broadcasted_iota(jnp.int32, (1, block_rows), 1)
    for b in range(blocks):
        square_tile = jnp.concatenate(
            [folded[b * most : (b + 1) * most], jnp.zeros((block_rows - most, LANES), F32)], axis=0
        )
        scores = jnp.sum(square_tile.T, axis=0, keepdims=True)
        out_ref[pl.ds(b, 1), :] = jnp.where(spot < count_ref[b], scores, 0.0)

    for copy in sends:
        copy.wait_send()


def solution(mesh):
    owners, parts = (mesh.shape[a] for a in ("users", "mp"))

    def local_fn(
        candidates,
        block_user,
        block_count,
        own_map,
        history_key_cache,
        cache_values,
        w_query_unit,
        time_bias,
        output_weight,
        w_score,
    ):
        blocks, block_rows, width = candidates.shape
        users_here, length, local = history_key_cache.shape
        heads = time_bias.shape[0]
        depth = output_weight.shape[0]
        rows = blocks * MOST
        dma = pltpu.SemaphoreType.DMA
        any_spec = pl.BlockSpec(memory_space=pl.ANY)
        return pl.pallas_call(
            functools.partial(kernel, (owners, parts)),
            out_shape=jax.ShapeDtypeStruct((blocks, block_rows), F32),
            in_specs=[any_spec] * 10,
            out_specs=pl.BlockSpec(memory_space=pltpu.VMEM),
            scratch_shapes=[
                pltpu.SMEM(block_user.shape, jnp.int32),
                pltpu.SMEM(block_count.shape, jnp.int32),
                pltpu.SMEM(own_map.shape, jnp.int32),
                pltpu.VMEM((blocks, MOST, width), BF16),
                pltpu.VMEM(w_query_unit.shape, BF16),
                pltpu.VMEM(history_key_cache.shape, BF16),
                pltpu.VMEM(cache_values.shape, BF16),
                pltpu.VMEM((depth, width), BF16),
                pltpu.VMEM((heads, length), F32),
                pltpu.VMEM((parts, 1, local), F32),
                pltpu.VMEM((blocks, MOST, local), BF16),
                pltpu.VMEM((owners, MOST, local), BF16),
                pltpu.VMEM((owners, MOST, local), BF16),
                pltpu.VMEM((owners, SUBLANES, LANES), jnp.int32),
                pltpu.VMEM((owners, SUBLANES, LANES), jnp.int32),
                pltpu.VMEM((rows, local), F32),
                pltpu.VMEM((owners, MOST, local), BF16),
                pltpu.VMEM((owners, MOST, local), BF16),
                pltpu.VMEM((owners, SUBLANES, LANES), F32),
                pltpu.VMEM((parts, owners, SUBLANES, LANES), F32),
                pltpu.VMEM((parts, rows, width), BF16),
                dma((blocks + 10,)),
                dma((owners,)),
                dma((owners,)),
                dma((owners,)),
                dma((owners,)),
                dma((owners,)),
                dma((owners,)),
                dma((parts, owners)),
                dma((parts, owners)),
                dma((parts,)),
                dma((parts,)),
                dma((parts,)),
                dma((parts,)),
            ],
            compiler_params=pltpu.CompilerParams(
                collective_id=0, has_side_effects=True, vmem_limit_bytes=32 * 1024 * 1024
            ),
        )(
            *(
                pltpu.with_memory_space_constraint(a, pltpu.HBM)
                for a in (
                    block_user,
                    block_count,
                    own_map,
                    candidates,
                    history_key_cache,
                    cache_values,
                    w_query_unit,
                    time_bias,
                    output_weight,
                    w_score.reshape(1, -1),
                )
            )
        )

    return jax.shard_map(
        local_fn,
        mesh=mesh,
        in_specs=(
            P(("groups", "users", "helpers"), None, None),
            P(("groups", "users", "helpers")),
            P(("groups", "users", "helpers")),
            P("groups"),
            P(("groups", "users"), None, "mp"),
            P(("groups", "users"), None, "mp"),
            P(None, None, "mp"),
            P("mp", None),
            P("mp", None),
            P("mp"),
        ),
        out_specs=P(("groups", "users", "helpers"), None),
        check_vma=False,
    )
```

```python
import functools

import jax
import jax.numpy as jnp
from jax import lax
from jax.experimental import pallas as pl
from jax.experimental.pallas import tpu as pltpu
from jax.sharding import PartitionSpec as P

EPSILON = 1e-05
MOST = 32
LANES = 128
SUBLANES = 8
MESH = pl.DeviceIdType.MESH
F32 = jnp.float32
BF16 = jnp.bfloat16


def silu(v):
    half = 0.5 * v
    return half + half * jnp.tanh(half)


def kernel(
    sizes,
    user_hbm,
    count_hbm,
    map_hbm,
    cand_ref,
    key_ref,
    value_ref,
    wqu_ref,
    bias_ref,
    wout_ref,
    wsc_ref,
    out_ref,
    user_ref,
    count_ref,
    map_ref,
    x_v,
    wqu_v,
    key_v,
    value_v,
    wout_v,
    bias_v,
    wsc_v,
    q_v,
    q_send,
    q_recv,
    tag_send,
    tag_recv,
    gate_v,
    mix_send,
    mix_recv,
    stat_send,
    stat_recv,
    part_v,
    load_sem,
    tag_ssem,
    tag_rsem,
    q_ssem,
    q_rsem,
    mix_ssem,
    mix_rsem,
    stat_ssem,
    stat_rsem,
    wsc_ssem,
    wsc_rsem,
    part_ssem,
    part_rsem,
):
    owners, parts = sizes
    u = lax.axis_index("users")
    m = lax.axis_index("mp")
    blocks, most, width = x_v.shape
    users_here, length, local = key_v.shape
    heads = bias_v.shape[0]
    head = local // heads
    rows = blocks * most
    tiles = most // SUBLANES

    def remote(src, dst, ssem, rsem, **device):
        return pltpu.make_async_remote_copy(
            src_ref=src,
            dst_ref=dst,
            send_sem=ssem,
            recv_sem=rsem,
            device_id=device,
            device_id_type=MESH,
        )

    def off(index, step, size):
        return lax.rem(index + step, size)

    def peer(k):
        return k + (k - u + owners) // owners

    barrier = pltpu.get_barrier_semaphore()
    for d in range(1, owners):
        pl.semaphore_signal(barrier, inc=1, device_id={"users": off(u, d, owners)}, device_id_type=MESH)
    for d in range(1, parts):
        pl.semaphore_signal(barrier, inc=1, device_id={"mp": off(m, d, parts)}, device_id_type=MESH)

    n = blocks
    scalars = [
        pltpu.make_async_copy(src, dst, load_sem.at[n + 7 + i])
        for i, (src, dst) in enumerate(
            ((user_hbm, user_ref), (map_hbm, map_ref), (count_hbm, count_ref))
        )
    ]
    loads = [pltpu.make_async_copy(cand_ref.at[b, pl.ds(0, most)], x_v.at[b], load_sem.at[b]) for b in range(blocks)]
    load_q = pltpu.make_async_copy(wqu_ref.at[0], wqu_v.at[0], load_sem.at[n])
    load_g = pltpu.make_async_copy(wqu_ref.at[1], wqu_v.at[1], load_sem.at[n + 1])
    load_k = pltpu.make_async_copy(key_ref, key_v, load_sem.at[n + 2])
    load_v = pltpu.make_async_copy(value_ref, value_v, load_sem.at[n + 3])
    load_w = pltpu.make_async_copy(wout_ref, wout_v, load_sem.at[n + 4])
    load_b = pltpu.make_async_copy(bias_ref, bias_v, load_sem.at[n + 5])
    load_s = pltpu.make_async_copy(wsc_ref, wsc_v.at[m], load_sem.at[n + 6])
    for load in scalars + loads + [load_q, load_g, load_b, load_k, load_v, load_s, load_w]:
        load.start()
    for load in scalars:
        load.wait()

    place = [map_ref[user_ref[b]] for b in range(blocks)]
    owner = [p // users_here for p in place]
    row = [p - o * users_here for p, o in zip(place, owner)]

    def routed(o):
        block, line = jnp.int32(0), jnp.int32(0)
        for b in range(blocks):
            hit = owner[b] == o
            block = jnp.where(hit, b, block)
            line = jnp.where(hit, row[b], line)
        return block, line

    targets = [u] + [peer(k) for k in range(owners - 1)]
    routes = [routed(o) for o in targets]
    for o, (block, line) in zip(targets, routes):
        tag_send[o] = jnp.full(tag_send.shape[1:], line, jnp.int32)

    for load in loads:
        load.wait()
    load_q.wait()
    x = x_v[...].reshape(rows, width)
    query = silu(jnp.dot(x, wqu_v[0], preferred_element_type=F32)).astype(BF16)
    q_v[...] = query.reshape(blocks, most, local)
    for d in range(1, owners):
        q_send[targets[d]] = q_v[routes[d][0]]

    pl.semaphore_wait(barrier, owners + parts - 2)

    sends = []

    def start(copy):
        copy.start()
        sends.append(copy)

    for d in reversed(range(1, owners)):
        o = targets[d]
        start(remote(q_send.at[o], q_recv.at[u], q_ssem.at[o], q_rsem.at[u], users=o))
        start(remote(tag_send.at[o], tag_recv.at[u], tag_ssem.at[o], tag_rsem.at[u], users=o))
    load_s.wait()
    for d in range(1, parts):
        p = off(m, d, parts)
        start(remote(wsc_v.at[m], wsc_v.at[m], wsc_ssem.at[p], wsc_rsem.at[m], mp=p))

    load_g.wait()
    gate_v[...] = silu(jnp.dot(x, wqu_v[1], preferred_element_type=F32))
    load_b.wait()
    load_k.wait()
    load_v.wait()
    scale = head ** (-0.5)
    lane = lax.broadcasted_iota(jnp.int32, (SUBLANES, LANES), 1)

    def attend(query_of, line):
        found = []
        for h in range(heads):
            cols = pl.ds(h * head, head)
            keys = key_v[line, :, cols]
            values = value_v[line, :, cols]
            logits = lax.dot_general(
                query_of(cols), keys, (((1,), (1,)), ((), ())), preferred_element_type=F32
            )
            weights = silu(logits * scale + bias_v[pl.ds(h, 1), :]).astype(BF16)
            found.append(jnp.dot(weights, values, preferred_element_type=F32))
        mean = jnp.sum(sum(found), axis=1, keepdims=True) / local
        centred = [f - mean for f in found]
        square = jnp.sum(sum(f * f for f in centred), axis=1, keepdims=True)
        stat = jnp.zeros((SUBLANES, LANES), F32)
        for t in range(tiles):
            part = slice(t * SUBLANES, (t + 1) * SUBLANES)
            stat = jnp.where(lane == t, mean[part], stat)
            stat = jnp.where(lane == tiles + t, square[part], stat)
        return [f.astype(BF16) for f in centred], stat

    def put(ref, index, pieces):
        for h in range(heads):
            ref[index, :, pl.ds(h * head, head)] = pieces[h]

    own_block, own_line = routes[0]
    pieces, stat = attend(lambda cols: q_v[own_block, :, cols], own_line)
    put(mix_recv, u, pieces)
    stat_recv[m, u] = stat
    for d in range(1, parts):
        p = off(m, d, parts)
        start(remote(stat_recv.at[m, u], stat_recv.at[m, u], stat_ssem.at[p, u], stat_rsem.at[m, u], mp=p))

    for d in range(1, owners):
        s = targets[d]
        remote(tag_send.at[s], tag_recv.at[s], tag_ssem.at[s], tag_rsem.at[s], users=s).wait_recv()
        remote(q_send.at[s], q_recv.at[s], q_ssem.at[s], q_rsem.at[s], users=s).wait_recv()
        line = tag_recv[s, 0, 0]
        pieces, stat = attend(lambda cols: q_recv[s, :, cols], line)
        put(mix_send, s, pieces)
        stat_send[s] = stat
        start(remote(mix_send.at[s], mix_recv.at[u], mix_ssem.at[s], mix_rsem.at[u], users=s))
        for e in range(parts):
            p = off(m, e, parts)
            start(remote(stat_send.at[s], stat_recv.at[m, u], stat_ssem.at[p, s], stat_rsem.at[m, u], users=s, mp=p))

    load_w.wait()
    for d in range(1, parts):
        p = off(m, d, parts)
        remote(wsc_v.at[p], wsc_v.at[p], wsc_ssem.at[p], wsc_rsem.at[p], mp=p).wait_recv()
    for d in range(owners):
        s = targets[d]
        for e in range(parts):
            if d or e:
                p = off(m, e, parts)
                remote(
                    stat_send.at[s], stat_recv.at[p, s], stat_ssem.at[p, s], stat_rsem.at[p, s], users=s, mp=p
                ).wait_recv()
        if d:
            remote(mix_send.at[s], mix_recv.at[s], mix_ssem.at[s], mix_rsem.at[s], users=s).wait_recv()

    gated = []
    for b in range(blocks):
        mine = mix_recv[owner[b]].astype(F32)
        means, squares = [], []
        for p in range(parts):
            stat = stat_recv[p, owner[b]]
            means.append(jnp.concatenate([stat[:, t : t + 1] for t in range(tiles)], axis=0))
            squares.append(jnp.concatenate([stat[:, tiles + t : tiles + t + 1] for t in range(tiles)], axis=0))
        row_mean = sum(means) / parts
        spread = sum(squares) / (parts * local) + sum((a - row_mean) * (a - row_mean) for a in means) / parts
        factor = lax.rsqrt(spread + EPSILON)
        stat = stat_recv[m, owner[b]]
        mean = jnp.concatenate([stat[:, t : t + 1] for t in range(tiles)], axis=0)
        gate = gate_v[pl.ds(b * most, most), :]
        gated.append(((mine + (mean - row_mean)) * factor * gate).astype(BF16))
    gated = jnp.concatenate(gated, axis=0)
    part_v[m] = jnp.dot(gated, wout_v[...], preferred_element_type=F32).astype(BF16)
    for d in range(1, parts):
        p = off(m, d, parts)
        start(remote(part_v.at[m], part_v.at[m], part_ssem.at[p], part_rsem.at[m], mp=p))
    for d in range(1, parts):
        p = off(m, d, parts)
        remote(part_v.at[p], part_v.at[p], part_ssem.at[p], part_rsem.at[p], mp=p).wait_recv()
    out_rows = part_v[0].astype(F32)
    for p in range(1, parts):
        out_rows = out_rows + part_v[p].astype(F32)
    shown = silu(x_v[...].reshape(rows, width).astype(F32) + out_rows)
    folded = jnp.zeros((rows, LANES), F32)
    for p in range(parts):
        for k in range(local // LANES):
            term = shown[:, p * local + k * LANES : p * local + (k + 1) * LANES]
            folded = folded + term * wsc_v[p, :, pl.ds(k * LANES, LANES)]
    block_rows = out_ref.shape[1]
    spot = lax.broadcasted_iota(jnp.int32, (1, block_rows), 1)
    for b in range(blocks):
        square_tile = jnp.concatenate(
            [folded[b * most : (b + 1) * most], jnp.zeros((block_rows - most, LANES), F32)], axis=0
        )
        scores = jnp.sum(square_tile.T, axis=0, keepdims=True)
        out_ref[pl.ds(b, 1), :] = jnp.where(spot < count_ref[b], scores, 0.0)

    for copy in sends:
        copy.wait_send()


def solution(mesh):
    owners, parts = (mesh.shape[a] for a in ("users", "mp"))

    def local_fn(
        candidates,
        block_user,
        block_count,
        own_map,
        history_key_cache,
        cache_values,
        w_query_unit,
        time_bias,
        output_weight,
        w_score,
    ):
        blocks, block_rows, width = candidates.shape
        users_here, length, local = history_key_cache.shape
        heads = time_bias.shape[0]
        depth = output_weight.shape[0]
        rows = blocks * MOST
        dma = pltpu.SemaphoreType.DMA
        any_spec = pl.BlockSpec(memory_space=pl.ANY)
        return pl.pallas_call(
            functools.partial(kernel, (owners, parts)),
            out_shape=jax.ShapeDtypeStruct((blocks, block_rows), F32),
            in_specs=[any_spec] * 10,
            out_specs=pl.BlockSpec(memory_space=pltpu.VMEM),
            scratch_shapes=[
                pltpu.SMEM(block_user.shape, jnp.int32),
                pltpu.SMEM(block_count.shape, jnp.int32),
                pltpu.SMEM(own_map.shape, jnp.int32),
                pltpu.VMEM((blocks, MOST, width), BF16),
                pltpu.VMEM(w_query_unit.shape, BF16),
                pltpu.VMEM(history_key_cache.shape, BF16),
                pltpu.VMEM(cache_values.shape, BF16),
                pltpu.VMEM((depth, width), BF16),
                pltpu.VMEM((heads, length), F32),
                pltpu.VMEM((parts, 1, local), F32),
                pltpu.VMEM((blocks, MOST, local), BF16),
                pltpu.VMEM((owners, MOST, local), BF16),
                pltpu.VMEM((owners, MOST, local), BF16),
                pltpu.VMEM((owners, SUBLANES, LANES), jnp.int32),
                pltpu.VMEM((owners, SUBLANES, LANES), jnp.int32),
                pltpu.VMEM((rows, local), F32),
                pltpu.VMEM((owners, MOST, local), BF16),
                pltpu.VMEM((owners, MOST, local), BF16),
                pltpu.VMEM((owners, SUBLANES, LANES), F32),
                pltpu.VMEM((parts, owners, SUBLANES, LANES), F32),
                pltpu.VMEM((parts, rows, width), BF16),
                dma((blocks + 10,)),
                dma((owners,)),
                dma((owners,)),
                dma((owners,)),
                dma((owners,)),
                dma((owners,)),
                dma((owners,)),
                dma((parts, owners)),
                dma((parts, owners)),
                dma((parts,)),
                dma((parts,)),
                dma((parts,)),
                dma((parts,)),
            ],
            compiler_params=pltpu.CompilerParams(
                collective_id=0, has_side_effects=True, vmem_limit_bytes=32 * 1024 * 1024
            ),
        )(
            *(
                pltpu.with_memory_space_constraint(a, pltpu.HBM)
                for a in (
                    block_user,
                    block_count,
                    own_map,
                    candidates,
                    history_key_cache,
                    cache_values,
                    w_query_unit,
                    time_bias,
                    output_weight,
                    w_score.reshape(1, -1),
                )
            )
        )

    return jax.shard_map(
        local_fn,
        mesh=mesh,
        in_specs=(
            P(("groups", "users", "helpers"), None, None),
            P(("groups", "users", "helpers")),
            P(("groups", "users", "helpers")),
            P("groups"),
            P(("groups", "users"), None, "mp"),
            P(("groups", "users"), None, "mp"),
            P(None, None, "mp"),
            P("mp", None),
            P("mp", None),
            P("mp"),
        ),
        out_specs=P(("groups", "users", "helpers"), None),
        check_vma=False,
    )
```

```python
import functools

import jax
import jax.numpy as jnp
from jax import lax
from jax.experimental import pallas as pl
from jax.experimental.pallas import tpu as pltpu
from jax.sharding import PartitionSpec as P

EPSILON = 1e-05
MOST = 32
LANES = 128
SUBLANES = 8
MESH = pl.DeviceIdType.MESH
F32 = jnp.float32
BF16 = jnp.bfloat16


def silu(v):
    half = 0.5 * v
    return half + half * jnp.tanh(half)


def kernel(
    sizes,
    user_hbm,
    count_hbm,
    map_hbm,
    cand_ref,
    key_ref,
    value_ref,
    wqu_ref,
    bias_ref,
    wout_ref,
    wsc_ref,
    out_ref,
    user_ref,
    count_ref,
    map_ref,
    x_v,
    wqu_v,
    key_v,
    value_v,
    wout_v,
    bias_v,
    wsc_v,
    q_v,
    q_send,
    q_recv,
    tag_send,
    tag_recv,
    gate_v,
    mix_send,
    mix_recv,
    stat_send,
    stat_recv,
    stat_v,
    base_v,
    part_v,
    rest_v,
    load_sem,
    tag_ssem,
    tag_rsem,
    q_ssem,
    q_rsem,
    mix_ssem,
    mix_rsem,
    stat_ssem,
    stat_rsem,
    wsc_ssem,
    wsc_rsem,
    norm_ssem,
    norm_rsem,
    base_ssem,
    base_rsem,
    part_ssem,
    part_rsem,
    user_ready,
    part_ready,
):
    owners, parts = sizes
    u = lax.axis_index("users")
    m = lax.axis_index("mp")
    blocks, most, width = x_v.shape
    users_here, length, local = key_v.shape
    heads = bias_v.shape[0]
    head = local // heads
    rows = blocks * most
    tiles = most // SUBLANES

    def remote(src, dst, ssem, rsem, **device):
        return pltpu.make_async_remote_copy(
            src_ref=src,
            dst_ref=dst,
            send_sem=ssem,
            recv_sem=rsem,
            device_id=device,
            device_id_type=MESH,
        )

    def off(index, step, size):
        return lax.rem(index + step, size)

    def peer(k):
        return k + (k - u + owners) // owners

    barrier = pltpu.get_barrier_semaphore()
    for o in range(owners):

        @pl.when(o > u)
        def _():
            pl.semaphore_signal(barrier, inc=1, device_id={"users": o}, device_id_type=MESH)

    for p in range(parts):

        @pl.when(p > m)
        def _():
            pl.semaphore_signal(barrier, inc=1, device_id={"mp": p}, device_id_type=MESH)


    @pl.when(u + m > 0)
    def _():
        pl.semaphore_wait(barrier, u + m)

    for o in range(owners):

        @pl.when(o < u)
        def _():
            pl.semaphore_signal(user_ready.at[u], inc=1, device_id={"users": o}, device_id_type=MESH)

    for p in range(parts):

        @pl.when(p < m)
        def _():
            pl.semaphore_signal(part_ready.at[m], inc=1, device_id={"mp": p}, device_id_type=MESH)

    def await_user(o):
        @pl.when(o > u)
        def _():
            pl.semaphore_wait(user_ready.at[o], 1)

    def await_parts():
        for p in range(parts):

            @pl.when(p > m)
            def _():
                pl.semaphore_wait(part_ready.at[p], 1)

    n = blocks
    scalars = [
        pltpu.make_async_copy(src, dst, load_sem.at[n + 7 + i])
        for i, (src, dst) in enumerate(
            ((user_hbm, user_ref), (map_hbm, map_ref), (count_hbm, count_ref))
        )
    ]
    loads = [pltpu.make_async_copy(cand_ref.at[b, pl.ds(0, most)], x_v.at[b], load_sem.at[b]) for b in range(blocks)]
    load_q = pltpu.make_async_copy(wqu_ref.at[0], wqu_v.at[0], load_sem.at[n])
    load_g = pltpu.make_async_copy(wqu_ref.at[1], wqu_v.at[1], load_sem.at[n + 1])
    load_k = pltpu.make_async_copy(key_ref, key_v, load_sem.at[n + 2])
    load_v = pltpu.make_async_copy(value_ref, value_v, load_sem.at[n + 3])
    load_w = pltpu.make_async_copy(wout_ref, wout_v, load_sem.at[n + 4])
    load_b = pltpu.make_async_copy(bias_ref, bias_v, load_sem.at[n + 5])
    load_s = pltpu.make_async_copy(wsc_ref, wsc_v.at[m], load_sem.at[n + 6])
    for load in scalars + loads + [load_q, load_s, load_b, load_g, load_w, load_k, load_v]:
        load.start()
    for load in scalars:
        load.wait()

    place = [map_ref[user_ref[b]] for b in range(blocks)]
    owner = [p // users_here for p in place]
    row = [p - o * users_here for p, o in zip(place, owner)]

    def routed(o):
        block, line = jnp.int32(0), jnp.int32(0)
        for b in range(blocks):
            hit = owner[b] == o
            block = jnp.where(hit, b, block)
            line = jnp.where(hit, row[b], line)
        return block, line

    targets = [u] + [peer(k) for k in range(owners - 1)]
    routes = [routed(o) for o in targets]
    for o, (block, line) in zip(targets, routes):
        tag_send[o] = jnp.full(tag_send.shape[1:], line, jnp.int32)

    for load in loads:
        load.wait()
    load_q.wait()
    x = x_v[...].reshape(rows, width)
    query = silu(jnp.dot(x, wqu_v[0], preferred_element_type=F32)).astype(BF16)
    q_v[...] = query.reshape(blocks, most, local)
    for d in range(1, owners):
        q_send[targets[d]] = q_v[routes[d][0]]

    sends = []

    def start(copy):
        copy.start()
        sends.append(copy)

    def send_query(d):
        o = targets[d]
        await_user(o)
        start(remote(q_send.at[o], q_recv.at[u], q_ssem.at[o], q_rsem.at[u], users=o))
        start(remote(tag_send.at[o], tag_recv.at[u], tag_ssem.at[o], tag_rsem.at[u], users=o))

    for d in range(1, owners - 1):
        send_query(d)
    load_g.wait()
    gate = silu(jnp.dot(x, wqu_v[1], preferred_element_type=F32))
    gate_v[...] = gate.reshape(blocks, most, local)
    load_w.wait()
    base_v[m] = jnp.dot(gate.astype(BF16), wout_v[...], preferred_element_type=F32).astype(BF16)
    for d in range(owners - 1, owners):
        send_query(d)
    load_s.wait()
    await_parts()
    for d in range(1, parts):
        p = off(m, d, parts)
        start(remote(wsc_v.at[m], wsc_v.at[m], wsc_ssem.at[p], wsc_rsem.at[m], mp=p))
        start(remote(base_v.at[m], base_v.at[m], base_ssem.at[p], base_rsem.at[m], mp=p))

    load_b.wait()
    load_k.wait()
    load_v.wait()
    scale = head ** (-0.5)
    lane = lax.broadcasted_iota(jnp.int32, (SUBLANES, LANES), 1)

    def attend(query_of, line):
        found = []
        for h in range(heads):
            cols = pl.ds(h * head, head)
            keys = key_v[line, :, cols]
            values = value_v[line, :, cols]
            logits = lax.dot_general(
                query_of(cols), keys, (((1,), (1,)), ((), ())), preferred_element_type=F32
            )
            weights = silu(logits * scale + bias_v[pl.ds(h, 1), :]).astype(BF16)
            found.append(jnp.dot(weights, values, preferred_element_type=F32))
        mean = jnp.sum(sum(found), axis=1, keepdims=True) / local
        centred = [f - mean for f in found]
        square = jnp.sum(sum(f * f for f in centred), axis=1, keepdims=True)
        stat = jnp.zeros((SUBLANES, LANES), F32)
        for t in range(tiles):
            part = slice(t * SUBLANES, (t + 1) * SUBLANES)
            stat = jnp.where(lane == t, mean[part], stat)
            stat = jnp.where(lane == tiles + t, square[part], stat)
        return [f.astype(BF16) for f in centred], stat

    def put(ref, index, pieces):
        for h in range(heads):
            ref[index, :, pl.ds(h * head, head)] = pieces[h]

    for d in range(1, owners):
        s = targets[d]
        remote(tag_send.at[s], tag_recv.at[s], tag_ssem.at[s], tag_rsem.at[s], users=s).wait_recv()
        remote(q_send.at[s], q_recv.at[s], q_ssem.at[s], q_rsem.at[s], users=s).wait_recv()
        line = tag_recv[s, 0, 0]
        pieces, stat = attend(lambda cols: q_recv[s, :, cols], line)
        put(mix_send, s, pieces)
        stat_send[s] = stat
        start(remote(mix_send.at[s], mix_recv.at[u], mix_ssem.at[s], mix_rsem.at[u], users=s))
        start(remote(stat_send.at[s], stat_recv.at[u], stat_ssem.at[s], stat_rsem.at[u], users=s))

    own_block, own_line = routes[0]
    pieces, stat = attend(lambda cols: q_v[own_block, :, cols], own_line)
    put(mix_recv, u, pieces)
    stat_recv[u] = stat

    def product(o, block):
        mixed = (mix_recv[o].astype(F32) * gate_v[block]).astype(BF16)
        part_v[m, o] = jnp.dot(mixed, wout_v[...], preferred_element_type=F32).astype(BF16)
        for d in range(1, parts):
            p = off(m, d, parts)
            start(remote(part_v.at[m, o], part_v.at[m, o], part_ssem.at[p, o], part_rsem.at[m, o], mp=p))

    product(u, own_block)
    for d in range(1, owners):
        s = targets[d]
        remote(mix_send.at[s], mix_recv.at[s], mix_ssem.at[s], mix_rsem.at[s], users=s).wait_recv()
        if d == owners - 1:
            for t in targets[1:]:
                remote(stat_send.at[t], stat_recv.at[t], stat_ssem.at[t], stat_rsem.at[t], users=t).wait_recv()
            for b in range(blocks):
                stat_v[m, b] = stat_recv[owner[b]]
            for e in range(1, parts):
                p = off(m, e, parts)
                start(remote(stat_v.at[m], stat_v.at[m], norm_ssem.at[p], norm_rsem.at[m], mp=p))
        product(s, routes[d][0])
    for d in range(1, parts):
        p = off(m, d, parts)
        remote(wsc_v.at[p], wsc_v.at[p], wsc_ssem.at[p], wsc_rsem.at[p], mp=p).wait_recv()
        remote(base_v.at[p], base_v.at[p], base_ssem.at[p], base_rsem.at[p], mp=p).wait_recv()
        remote(stat_v.at[p], stat_v.at[p], norm_ssem.at[p], norm_rsem.at[p], mp=p).wait_recv()

    def column(tiled):
        return jnp.concatenate([tiled[b][:, t : t + 1] for b in range(blocks) for t in range(tiles)], axis=0)

    stats = [[stat_v[p, b] for b in range(blocks)] for p in range(parts)]
    row_mean = [sum(stats[p][b] for p in range(parts)) / parts for b in range(blocks)]
    factor = []
    for b in range(blocks):
        spread = pltpu.roll(row_mean[b], LANES - tiles, 1) / local
        for p in range(parts):
            shift = stats[p][b] - row_mean[b]
            spread = spread + shift * shift / parts
        factor.append(lax.rsqrt(spread + EPSILON))
    factor = column(factor)
    base = jnp.zeros((rows, width), F32)
    for p in range(parts):
        shift = column([stats[p][b] - row_mean[b] for b in range(blocks)])
        base = base + shift * base_v[p].astype(F32)
    rest_v[...] = x_v[...].reshape(rows, width).astype(F32) + base * factor
    for d in range(1, parts):
        p = off(m, d, parts)
        for o in targets:
            remote(part_v.at[p, o], part_v.at[p, o], part_ssem.at[p, o], part_rsem.at[p, o], mp=p).wait_recv()
    part = jnp.concatenate(
        [sum(part_v[p, owner[b]].astype(F32) for p in range(parts)) for b in range(blocks)], axis=0
    )
    shown = silu(rest_v[...] + part * factor)
    folded = jnp.zeros((rows, LANES), F32)
    for p in range(parts):
        for k in range(local // LANES):
            term = shown[:, p * local + k * LANES : p * local + (k + 1) * LANES]
            folded = folded + term * wsc_v[p, :, pl.ds(k * LANES, LANES)]
    block_rows = out_ref.shape[1]
    spot = lax.broadcasted_iota(jnp.int32, (1, block_rows), 1)
    for b in range(blocks):
        square_tile = jnp.concatenate(
            [folded[b * most : (b + 1) * most], jnp.zeros((block_rows - most, LANES), F32)], axis=0
        )
        scores = jnp.sum(square_tile.T, axis=0, keepdims=True)
        out_ref[pl.ds(b, 1), :] = jnp.where(spot < count_ref[b], scores, 0.0)

    for copy in sends:
        copy.wait_send()


def solution(mesh):
    owners, parts = (mesh.shape[a] for a in ("users", "mp"))

    def local_fn(
        candidates,
        block_user,
        block_count,
        own_map,
        history_key_cache,
        cache_values,
        w_query_unit,
        time_bias,
        output_weight,
        w_score,
    ):
        blocks, block_rows, width = candidates.shape
        users_here, length, local = history_key_cache.shape
        heads = time_bias.shape[0]
        depth = output_weight.shape[0]
        rows = blocks * MOST
        dma = pltpu.SemaphoreType.DMA
        any_spec = pl.BlockSpec(memory_space=pl.ANY)
        return pl.pallas_call(
            functools.partial(kernel, (owners, parts)),
            out_shape=jax.ShapeDtypeStruct((blocks, block_rows), F32),
            in_specs=[any_spec] * 10,
            out_specs=pl.BlockSpec(memory_space=pltpu.VMEM),
            scratch_shapes=[
                pltpu.SMEM(block_user.shape, jnp.int32),
                pltpu.SMEM(block_count.shape, jnp.int32),
                pltpu.SMEM(own_map.shape, jnp.int32),
                pltpu.VMEM((blocks, MOST, width), BF16),
                pltpu.VMEM(w_query_unit.shape, BF16),
                pltpu.VMEM(history_key_cache.shape, BF16),
                pltpu.VMEM(cache_values.shape, BF16),
                pltpu.VMEM((depth, width), BF16),
                pltpu.VMEM((heads, length), F32),
                pltpu.VMEM((parts, 1, local), F32),
                pltpu.VMEM((blocks, MOST, local), BF16),
                pltpu.VMEM((owners, MOST, local), BF16),
                pltpu.VMEM((owners, MOST, local), BF16),
                pltpu.VMEM((owners, SUBLANES, LANES), jnp.int32),
                pltpu.VMEM((owners, SUBLANES, LANES), jnp.int32),
                pltpu.VMEM((blocks, MOST, local), F32),
                pltpu.VMEM((owners, MOST, local), BF16),
                pltpu.VMEM((owners, MOST, local), BF16),
                pltpu.VMEM((owners, SUBLANES, LANES), F32),
                pltpu.VMEM((owners, SUBLANES, LANES), F32),
                pltpu.VMEM((parts, blocks, SUBLANES, LANES), F32),
                pltpu.VMEM((parts, rows, width), BF16),
                pltpu.VMEM((parts, owners, MOST, width), BF16),
                pltpu.VMEM((rows, width), F32),
                dma((blocks + 10,)),
                dma((owners,)),
                dma((owners,)),
                dma((owners,)),
                dma((owners,)),
                dma((owners,)),
                dma((owners,)),
                dma((owners,)),
                dma((owners,)),
                dma((parts,)),
                dma((parts,)),
                dma((parts,)),
                dma((parts,)),
                dma((parts,)),
                dma((parts,)),
                dma((parts, owners)),
                dma((parts, owners)),
                pltpu.SemaphoreType.REGULAR((owners,)),
                pltpu.SemaphoreType.REGULAR((parts,)),
            ],
            compiler_params=pltpu.CompilerParams(
                collective_id=0, has_side_effects=True, vmem_limit_bytes=32 * 1024 * 1024
            ),
        )(
            *(
                pltpu.with_memory_space_constraint(a, pltpu.HBM)
                for a in (
                    block_user,
                    block_count,
                    own_map,
                    candidates,
                    history_key_cache,
                    cache_values,
                    w_query_unit,
                    time_bias,
                    output_weight,
                    w_score.reshape(1, -1),
                )
            )
        )

    return jax.shard_map(
        local_fn,
        mesh=mesh,
        in_specs=(
            P(("groups", "users", "helpers"), None, None),
            P(("groups", "users", "helpers")),
            P(("groups", "users", "helpers")),
            P("groups"),
            P(("groups", "users"), None, "mp"),
            P(("groups", "users"), None, "mp"),
            P(None, None, "mp"),
            P("mp", None),
            P("mp", None),
            P("mp"),
        ),
        out_specs=P(("groups", "users", "helpers"), None),
        check_vma=False,
    )
```

```python
import functools

import jax
import jax.numpy as jnp
from jax import lax
from jax.experimental import pallas as pl
from jax.experimental.pallas import tpu as pltpu
from jax.sharding import PartitionSpec as P

EPSILON = 1e-05
MOST = 32
LANES = 128
SUBLANES = 8
MESH = pl.DeviceIdType.MESH
F32 = jnp.float32
BF16 = jnp.bfloat16


def silu(v):
    half = 0.5 * v
    return half + half * jnp.tanh(half)


def kernel(
    sizes,
    user_hbm,
    count_hbm,
    map_hbm,
    cand_ref,
    key_ref,
    value_ref,
    wqu_ref,
    bias_ref,
    wout_ref,
    wsc_ref,
    out_ref,
    user_ref,
    count_ref,
    map_ref,
    x_v,
    wqu_v,
    key_v,
    value_v,
    wout_v,
    bias_v,
    wsc_v,
    q_v,
    q_send,
    q_recv,
    tag_send,
    tag_recv,
    gate_v,
    mix_send,
    mix_recv,
    stat_send,
    stat_recv,
    stat_v,
    base_v,
    part_v,
    rest_v,
    load_sem,
    tag_ssem,
    tag_rsem,
    q_ssem,
    q_rsem,
    mix_ssem,
    mix_rsem,
    stat_ssem,
    stat_rsem,
    wsc_ssem,
    wsc_rsem,
    norm_ssem,
    norm_rsem,
    base_ssem,
    base_rsem,
    part_ssem,
    part_rsem,
    user_ready,
    part_ready,
):
    owners, parts = sizes
    u = lax.axis_index("users")
    m = lax.axis_index("mp")
    blocks, most, width = x_v.shape
    users_here, length, local = key_v.shape
    heads = bias_v.shape[0]
    head = local // heads
    rows = blocks * most
    tiles = most // SUBLANES

    def remote(src, dst, ssem, rsem, **device):
        return pltpu.make_async_remote_copy(
            src_ref=src,
            dst_ref=dst,
            send_sem=ssem,
            recv_sem=rsem,
            device_id=device,
            device_id_type=MESH,
        )

    def off(index, step, size):
        return lax.rem(index + step, size)

    def peer(k):
        return k + (k - u + owners) // owners

    barrier = pltpu.get_barrier_semaphore()
    for o in range(owners):

        @pl.when(o > u)
        def _():
            pl.semaphore_signal(barrier, inc=1, device_id={"users": o}, device_id_type=MESH)

    for p in range(parts):

        @pl.when(p > m)
        def _():
            pl.semaphore_signal(barrier, inc=1, device_id={"mp": p}, device_id_type=MESH)


    @pl.when(u + m > 0)
    def _():
        pl.semaphore_wait(barrier, u + m)

    for o in range(owners):

        @pl.when(o < u)
        def _():
            pl.semaphore_signal(user_ready.at[u], inc=1, device_id={"users": o}, device_id_type=MESH)

    for p in range(parts):

        @pl.when(p < m)
        def _():
            pl.semaphore_signal(part_ready.at[m], inc=1, device_id={"mp": p}, device_id_type=MESH)

    def await_user(o):
        @pl.when(o > u)
        def _():
            pl.semaphore_wait(user_ready.at[o], 1)

    def await_parts():
        for p in range(parts):

            @pl.when(p > m)
            def _():
                pl.semaphore_wait(part_ready.at[p], 1)

    n = blocks
    scalars = [
        pltpu.make_async_copy(src, dst, load_sem.at[n + 7 + i])
        for i, (src, dst) in enumerate(
            ((user_hbm, user_ref), (map_hbm, map_ref), (count_hbm, count_ref))
        )
    ]
    loads = [pltpu.make_async_copy(cand_ref.at[b, pl.ds(0, most)], x_v.at[b], load_sem.at[b]) for b in range(blocks)]
    load_q = pltpu.make_async_copy(wqu_ref.at[0], wqu_v.at[0], load_sem.at[n])
    load_g = pltpu.make_async_copy(wqu_ref.at[1], wqu_v.at[1], load_sem.at[n + 1])
    load_k = pltpu.make_async_copy(key_ref, key_v, load_sem.at[n + 2])
    load_v = pltpu.make_async_copy(value_ref, value_v, load_sem.at[n + 3])
    load_w = pltpu.make_async_copy(wout_ref, wout_v, load_sem.at[n + 4])
    load_b = pltpu.make_async_copy(bias_ref, bias_v, load_sem.at[n + 5])
    load_s = pltpu.make_async_copy(wsc_ref, wsc_v.at[m], load_sem.at[n + 6])
    for load in scalars + loads + [load_q, load_s, load_b, load_g, load_w, load_k, load_v]:
        load.start()
    for load in scalars:
        load.wait()

    place = [map_ref[user_ref[b]] for b in range(blocks)]
    owner = [p // users_here for p in place]
    row = [p - o * users_here for p, o in zip(place, owner)]

    def routed(o):
        block, line = jnp.int32(0), jnp.int32(0)
        for b in range(blocks):
            hit = owner[b] == o
            block = jnp.where(hit, b, block)
            line = jnp.where(hit, row[b], line)
        return block, line

    targets = [u] + [peer(k) for k in range(owners - 1)]
    routes = [routed(o) for o in targets]
    for o, (block, line) in zip(targets, routes):
        tag_send[o] = jnp.full(tag_send.shape[1:], line, jnp.int32)

    for load in loads:
        load.wait()
    load_q.wait()
    x = x_v[...].reshape(rows, width)
    query = silu(jnp.dot(x, wqu_v[0], preferred_element_type=F32)).astype(BF16)
    q_v[...] = query.reshape(blocks, most, local)
    for d in range(1, owners):
        q_send[targets[d]] = q_v[routes[d][0]]

    sends = []

    def start(copy):
        copy.start()
        sends.append(copy)

    def send_query(d):
        o = targets[d]
        await_user(o)
        start(remote(tag_send.at[o], tag_recv.at[u], tag_ssem.at[o], tag_rsem.at[u], users=o))
        start(remote(q_send.at[o], q_recv.at[u], q_ssem.at[o], q_rsem.at[u], users=o))

    for d in range(1, owners - 1):
        send_query(d)
    load_g.wait()
    gate = silu(jnp.dot(x, wqu_v[1], preferred_element_type=F32))
    gate_v[...] = gate.reshape(blocks, most, local)
    load_w.wait()
    base_v[m] = jnp.dot(gate.astype(BF16), wout_v[...], preferred_element_type=F32).astype(BF16)
    for d in range(owners - 1, owners):
        send_query(d)
    load_s.wait()
    await_parts()
    for d in range(1, parts):
        p = off(m, d, parts)
        start(remote(wsc_v.at[m], wsc_v.at[m], wsc_ssem.at[p], wsc_rsem.at[m], mp=p))
        start(remote(base_v.at[m], base_v.at[m], base_ssem.at[p], base_rsem.at[m], mp=p))

    load_b.wait()
    load_k.wait()
    load_v.wait()
    scale = head ** (-0.5)
    lane = lax.broadcasted_iota(jnp.int32, (SUBLANES, LANES), 1)

    def attend(query, line):
        found = []
        for h in range(heads):
            cols = pl.ds(h * head, head)
            logits = lax.dot_general(
                query[:, h * head : (h + 1) * head], key_v[line, :, cols], (((1,), (1,)), ((), ())), preferred_element_type=F32
            )
            half = logits * (0.5 * scale) + 0.5 * bias_v[pl.ds(h, 1), :]
            found.append((half + half * jnp.tanh(half)).astype(BF16))
        mixed = jnp.dot(jnp.concatenate(found, axis=0), value_v[line], preferred_element_type=F32)
        found = [mixed[h * most : (h + 1) * most, h * head : (h + 1) * head] for h in range(heads)]
        mean = jnp.sum(sum(found), axis=1, keepdims=True) / local
        return [f - mean for f in found], mean

    def put(ref, index, centred):
        for h in range(heads):
            ref[index, :, pl.ds(h * head, head)] = centred[h].astype(BF16)

    def statistics(ref, index, centred, mean):
        square = jnp.sum(sum(f * f for f in centred), axis=1, keepdims=True)
        stat = jnp.zeros((SUBLANES, LANES), F32)
        for t in range(tiles):
            part = slice(t * SUBLANES, (t + 1) * SUBLANES)
            stat = jnp.where(lane == t, mean[part], stat)
            stat = jnp.where(lane == tiles + t, square[part], stat)
        ref[index] = stat

    for d in range(1, owners):
        s = targets[d]
        remote(tag_send.at[s], tag_recv.at[s], tag_ssem.at[s], tag_rsem.at[s], users=s).wait_recv()
        line = tag_recv[s, 0, 0]
        remote(q_send.at[s], q_recv.at[s], q_ssem.at[s], q_rsem.at[s], users=s).wait_recv()
        centred, mean = attend(q_recv[s], line)
        put(mix_send, s, centred)
        start(remote(mix_send.at[s], mix_recv.at[u], mix_ssem.at[s], mix_rsem.at[u], users=s))
        statistics(stat_send, s, centred, mean)
        start(remote(stat_send.at[s], stat_recv.at[u], stat_ssem.at[s], stat_rsem.at[u], users=s))

    own_block, own_line = routes[0]
    centred, mean = attend(q_v[own_block], own_line)
    put(mix_recv, u, centred)
    statistics(stat_recv, u, centred, mean)

    def product(o, block):
        mixed = (mix_recv[o].astype(F32) * gate_v[block]).astype(BF16)
        part_v[m, o] = jnp.dot(mixed, wout_v[...], preferred_element_type=F32).astype(BF16)
        for d in range(1, parts):
            p = off(m, d, parts)
            start(remote(part_v.at[m, o], part_v.at[m, o], part_ssem.at[p, o], part_rsem.at[m, o], mp=p))

    product(u, own_block)
    for d in range(1, owners):
        s = targets[d]
        remote(mix_send.at[s], mix_recv.at[s], mix_ssem.at[s], mix_rsem.at[s], users=s).wait_recv()
        if d == owners - 1:
            for t in targets[1:]:
                remote(stat_send.at[t], stat_recv.at[t], stat_ssem.at[t], stat_rsem.at[t], users=t).wait_recv()
            for b in range(blocks):
                stat_v[m, b] = stat_recv[owner[b]]
            for e in range(1, parts):
                p = off(m, e, parts)
                start(remote(stat_v.at[m], stat_v.at[m], norm_ssem.at[p], norm_rsem.at[m], mp=p))
        product(s, routes[d][0])
    for d in range(1, parts):
        p = off(m, d, parts)
        remote(wsc_v.at[p], wsc_v.at[p], wsc_ssem.at[p], wsc_rsem.at[p], mp=p).wait_recv()
        remote(base_v.at[p], base_v.at[p], base_ssem.at[p], base_rsem.at[p], mp=p).wait_recv()
        remote(stat_v.at[p], stat_v.at[p], norm_ssem.at[p], norm_rsem.at[p], mp=p).wait_recv()

    def column(tiled):
        return jnp.concatenate([tiled[b][:, t : t + 1] for b in range(blocks) for t in range(tiles)], axis=0)

    stats = [[stat_v[p, b] for b in range(blocks)] for p in range(parts)]
    row_mean = [sum(stats[p][b] for p in range(parts)) / parts for b in range(blocks)]
    factor = []
    for b in range(blocks):
        spread = pltpu.roll(row_mean[b], LANES - tiles, 1) / local
        for p in range(parts):
            shift = stats[p][b] - row_mean[b]
            spread = spread + shift * shift / parts
        factor.append(lax.rsqrt(spread + EPSILON))
    factor = column(factor)
    base = jnp.zeros((rows, width), F32)
    for p in range(parts):
        shift = column([stats[p][b] - row_mean[b] for b in range(blocks)])
        base = base + shift * base_v[p].astype(F32)
    rest_v[...] = x_v[...].reshape(rows, width).astype(F32) + base * factor
    for d in range(1, parts):
        p = off(m, d, parts)
        for o in targets:
            remote(part_v.at[p, o], part_v.at[p, o], part_ssem.at[p, o], part_rsem.at[p, o], mp=p).wait_recv()
    part = jnp.concatenate(
        [sum(part_v[p, owner[b]].astype(F32) for p in range(parts)) for b in range(blocks)], axis=0
    )
    shown = silu(rest_v[...] + part * factor)
    folded = jnp.zeros((rows, LANES), F32)
    for p in range(parts):
        for k in range(local // LANES):
            term = shown[:, p * local + k * LANES : p * local + (k + 1) * LANES]
            folded = folded + term * wsc_v[p, :, pl.ds(k * LANES, LANES)]
    block_rows = out_ref.shape[1]
    spot = lax.broadcasted_iota(jnp.int32, (1, block_rows), 1)
    for b in range(blocks):
        square_tile = jnp.concatenate(
            [folded[b * most : (b + 1) * most], jnp.zeros((block_rows - most, LANES), F32)], axis=0
        )
        scores = jnp.sum(square_tile.T, axis=0, keepdims=True)
        out_ref[pl.ds(b, 1), :] = jnp.where(spot < count_ref[b], scores, 0.0)

    for copy in sends:
        copy.wait_send()


def solution(mesh):
    owners, parts = (mesh.shape[a] for a in ("users", "mp"))

    def local_fn(
        candidates,
        block_user,
        block_count,
        own_map,
        history_key_cache,
        cache_values,
        w_query_unit,
        time_bias,
        output_weight,
        w_score,
    ):
        blocks, block_rows, width = candidates.shape
        users_here, length, local = history_key_cache.shape
        heads = time_bias.shape[0]
        depth = output_weight.shape[0]
        rows = blocks * MOST
        dma = pltpu.SemaphoreType.DMA
        any_spec = pl.BlockSpec(memory_space=pl.ANY)
        return pl.pallas_call(
            functools.partial(kernel, (owners, parts)),
            out_shape=jax.ShapeDtypeStruct((blocks, block_rows), F32),
            in_specs=[any_spec] * 10,
            out_specs=pl.BlockSpec(memory_space=pltpu.VMEM),
            scratch_shapes=[
                pltpu.SMEM(block_user.shape, jnp.int32),
                pltpu.SMEM(block_count.shape, jnp.int32),
                pltpu.SMEM(own_map.shape, jnp.int32),
                pltpu.VMEM((blocks, MOST, width), BF16),
                pltpu.VMEM(w_query_unit.shape, BF16),
                pltpu.VMEM(history_key_cache.shape, BF16),
                pltpu.VMEM(cache_values.shape, BF16),
                pltpu.VMEM((depth, width), BF16),
                pltpu.VMEM((heads, length), F32),
                pltpu.VMEM((parts, 1, local), F32),
                pltpu.VMEM((blocks, MOST, local), BF16),
                pltpu.VMEM((owners, MOST, local), BF16),
                pltpu.VMEM((owners, MOST, local), BF16),
                pltpu.VMEM((owners, SUBLANES, LANES), jnp.int32),
                pltpu.VMEM((owners, SUBLANES, LANES), jnp.int32),
                pltpu.VMEM((blocks, MOST, local), F32),
                pltpu.VMEM((owners, MOST, local), BF16),
                pltpu.VMEM((owners, MOST, local), BF16),
                pltpu.VMEM((owners, SUBLANES, LANES), F32),
                pltpu.VMEM((owners, SUBLANES, LANES), F32),
                pltpu.VMEM((parts, blocks, SUBLANES, LANES), F32),
                pltpu.VMEM((parts, rows, width), BF16),
                pltpu.VMEM((parts, owners, MOST, width), BF16),
                pltpu.VMEM((rows, width), F32),
                dma((blocks + 10,)),
                dma((owners,)),
                dma((owners,)),
                dma((owners,)),
                dma((owners,)),
                dma((owners,)),
                dma((owners,)),
                dma((owners,)),
                dma((owners,)),
                dma((parts,)),
                dma((parts,)),
                dma((parts,)),
                dma((parts,)),
                dma((parts,)),
                dma((parts,)),
                dma((parts, owners)),
                dma((parts, owners)),
                pltpu.SemaphoreType.REGULAR((owners,)),
                pltpu.SemaphoreType.REGULAR((parts,)),
            ],
            compiler_params=pltpu.CompilerParams(
                collective_id=0, has_side_effects=True, vmem_limit_bytes=32 * 1024 * 1024
            ),
        )(
            *(
                pltpu.with_memory_space_constraint(a, pltpu.HBM)
                for a in (
                    block_user,
                    block_count,
                    own_map,
                    candidates,
                    history_key_cache,
                    cache_values,
                    w_query_unit,
                    time_bias,
                    output_weight,
                    w_score.reshape(1, -1),
                )
            )
        )

    return jax.shard_map(
        local_fn,
        mesh=mesh,
        in_specs=(
            P(("groups", "users", "helpers"), None, None),
            P(("groups", "users", "helpers")),
            P(("groups", "users", "helpers")),
            P("groups"),
            P(("groups", "users"), None, "mp"),
            P(("groups", "users"), None, "mp"),
            P(None, None, "mp"),
            P("mp", None),
            P("mp", None),
            P("mp"),
        ),
        out_specs=P(("groups", "users", "helpers"), None),
        check_vma=False,
    )
```

```python
import functools

import jax
import jax.numpy as jnp
from jax import lax
from jax.experimental import pallas as pl
from jax.experimental.pallas import tpu as pltpu
from jax.sharding import PartitionSpec as P

EPSILON = 1e-05
MOST = 32
LANES = 128
SUBLANES = 8
MESH = pl.DeviceIdType.MESH
F32 = jnp.float32
BF16 = jnp.bfloat16


def silu(v):
    half = 0.5 * v
    return half + half * jnp.tanh(half)


def kernel(
    sizes,
    user_hbm,
    count_hbm,
    map_hbm,
    cand_ref,
    key_ref,
    value_ref,
    wqu_ref,
    bias_ref,
    wout_ref,
    wsc_ref,
    out_ref,
    user_ref,
    count_ref,
    map_ref,
    x_v,
    wqu_v,
    key_v,
    value_v,
    wout_v,
    bias_v,
    wsc_v,
    q_v,
    q_send,
    q_recv,
    tag_send,
    tag_recv,
    gate_v,
    mix_send,
    mix_recv,
    stat_send,
    stat_recv,
    stat_v,
    base_v,
    part_v,
    rest_v,
    load_sem,
    tag_ssem,
    tag_rsem,
    q_ssem,
    q_rsem,
    mix_ssem,
    mix_rsem,
    stat_ssem,
    stat_rsem,
    wsc_ssem,
    wsc_rsem,
    norm_ssem,
    norm_rsem,
    base_ssem,
    base_rsem,
    part_ssem,
    part_rsem,
    user_ready,
    part_ready,
):
    owners, parts = sizes
    u = lax.axis_index("users")
    m = lax.axis_index("mp")
    blocks, most, width = x_v.shape
    users_here, length, local = key_v.shape
    heads = bias_v.shape[0]
    head = local // heads
    rows = blocks * most
    tiles = most // SUBLANES

    def remote(src, dst, ssem, rsem, **device):
        return pltpu.make_async_remote_copy(
            src_ref=src,
            dst_ref=dst,
            send_sem=ssem,
            recv_sem=rsem,
            device_id=device,
            device_id_type=MESH,
        )

    def off(index, step, size):
        return lax.rem(index + step, size)

    def peer(k):
        return k + (k - u + owners) // owners

    barrier = pltpu.get_barrier_semaphore()
    for o in range(owners):

        @pl.when(o > u)
        def _():
            pl.semaphore_signal(barrier, inc=1, device_id={"users": o}, device_id_type=MESH)

    for p in range(parts):

        @pl.when(p > m)
        def _():
            pl.semaphore_signal(barrier, inc=1, device_id={"mp": p}, device_id_type=MESH)


    @pl.when(u + m > 0)
    def _():
        pl.semaphore_wait(barrier, u + m)

    for o in range(owners):

        @pl.when(o < u)
        def _():
            pl.semaphore_signal(user_ready.at[u], inc=1, device_id={"users": o}, device_id_type=MESH)

    for p in range(parts):

        @pl.when(p < m)
        def _():
            pl.semaphore_signal(part_ready.at[m], inc=1, device_id={"mp": p}, device_id_type=MESH)

    def await_user(o):
        @pl.when(o > u)
        def _():
            pl.semaphore_wait(user_ready.at[o], 1)

    def await_parts():
        for p in range(parts):

            @pl.when(p > m)
            def _():
                pl.semaphore_wait(part_ready.at[p], 1)

    n = blocks
    scalars = [
        pltpu.make_async_copy(src, dst, load_sem.at[n + 7 + i])
        for i, (src, dst) in enumerate(
            ((user_hbm, user_ref), (map_hbm, map_ref), (count_hbm, count_ref))
        )
    ]
    loads = [pltpu.make_async_copy(cand_ref.at[b, pl.ds(0, most)], x_v.at[b], load_sem.at[b]) for b in range(blocks)]
    load_q = pltpu.make_async_copy(wqu_ref.at[0], wqu_v.at[0], load_sem.at[n])
    load_g = pltpu.make_async_copy(wqu_ref.at[1], wqu_v.at[1], load_sem.at[n + 1])
    load_k = pltpu.make_async_copy(key_ref, key_v, load_sem.at[n + 2])
    load_v = pltpu.make_async_copy(value_ref, value_v, load_sem.at[n + 3])
    load_w = pltpu.make_async_copy(wout_ref, wout_v, load_sem.at[n + 4])
    load_b = pltpu.make_async_copy(bias_ref, bias_v, load_sem.at[n + 5])
    load_s = pltpu.make_async_copy(wsc_ref, wsc_v.at[m], load_sem.at[n + 6])
    for load in scalars + loads + [load_q, load_s, load_b, load_g, load_w, load_k, load_v]:
        load.start()
    for load in scalars:
        load.wait()

    place = [map_ref[user_ref[b]] for b in range(blocks)]
    owner = [p // users_here for p in place]
    row = [p - o * users_here for p, o in zip(place, owner)]

    def routed(o):
        block, line = jnp.int32(0), jnp.int32(0)
        for b in range(blocks):
            hit = owner[b] == o
            block = jnp.where(hit, b, block)
            line = jnp.where(hit, row[b], line)
        return block, line

    targets = [u] + [peer(k) for k in range(owners - 1)]
    routes = [routed(o) for o in targets]
    for o, (block, line) in zip(targets, routes):
        tag_send[o] = jnp.full(tag_send.shape[1:], line, jnp.int32)

    for load in loads:
        load.wait()
    load_q.wait()
    x = x_v[...].reshape(rows, width)
    query = silu(jnp.dot(x, wqu_v[0], preferred_element_type=F32)).astype(BF16)
    q_v[...] = query.reshape(blocks, most, local)
    for d in range(1, owners):
        q_send[targets[d]] = q_v[routes[d][0]]

    sends = []

    def start(copy):
        copy.start()
        sends.append(copy)

    def send_query(d):
        o = targets[d]
        await_user(o)
        start(remote(tag_send.at[o], tag_recv.at[u], tag_ssem.at[o], tag_rsem.at[u], users=o))
        start(remote(q_send.at[o], q_recv.at[u], q_ssem.at[o], q_rsem.at[u], users=o))

    for d in range(1, owners - 1):
        send_query(d)
    load_g.wait()
    gate = silu(jnp.dot(x, wqu_v[1], preferred_element_type=F32))
    gate_v[...] = gate.reshape(blocks, most, local)
    load_w.wait()
    base_v[m] = jnp.dot(gate.astype(BF16), wout_v[...], preferred_element_type=F32).astype(BF16)
    for d in range(owners - 1, owners):
        send_query(d)
    load_s.wait()
    await_parts()
    for d in range(1, parts):
        p = off(m, d, parts)
        start(remote(wsc_v.at[m], wsc_v.at[m], wsc_ssem.at[p], wsc_rsem.at[m], mp=p))
        start(remote(base_v.at[m], base_v.at[m], base_ssem.at[p], base_rsem.at[m], mp=p))

    load_b.wait()
    load_k.wait()
    load_v.wait()
    scale = head ** (-0.5)
    lane = lax.broadcasted_iota(jnp.int32, (SUBLANES, LANES), 1)

    def attend(query, line):
        found = []
        for h in range(heads):
            cols = pl.ds(h * head, head)
            logits = lax.dot_general(
                query[:, h * head : (h + 1) * head], key_v[line, :, cols], (((1,), (1,)), ((), ())), preferred_element_type=F32
            )
            half = logits * (0.5 * scale) + 0.5 * bias_v[pl.ds(h, 1), :]
            found.append((half + half * jnp.tanh(half)).astype(BF16))
        mixed = jnp.dot(jnp.concatenate(found, axis=0), value_v[line], preferred_element_type=F32)
        found = [mixed[h * most : (h + 1) * most, h * head : (h + 1) * head] for h in range(heads)]
        mean = jnp.sum(sum(found), axis=1, keepdims=True) / local
        return [f - mean for f in found], mean

    def put(ref, index, centred):
        for h in range(heads):
            ref[index, :, pl.ds(h * head, head)] = centred[h].astype(BF16)

    def statistics(ref, index, centred, mean):
        square = jnp.sum(sum(f * f for f in centred), axis=1, keepdims=True)
        stat = jnp.zeros((SUBLANES, LANES), F32)
        for t in range(tiles):
            part = slice(t * SUBLANES, (t + 1) * SUBLANES)
            stat = jnp.where(lane == t, mean[part], stat)
            stat = jnp.where(lane == tiles + t, square[part], stat)
        ref[index] = stat

    own_block, own_line = routes[0]

    def own_slot():
        centred, mean = attend(q_v[own_block], own_line)
        put(mix_recv, u, centred)
        statistics(stat_recv, u, centred, mean)

    pl.when(u == 0)(own_slot)
    for d in range(1, owners):
        s = targets[d]
        remote(tag_send.at[s], tag_recv.at[s], tag_ssem.at[s], tag_rsem.at[s], users=s).wait_recv()
        line = tag_recv[s, 0, 0]
        remote(q_send.at[s], q_recv.at[s], q_ssem.at[s], q_rsem.at[s], users=s).wait_recv()
        centred, mean = attend(q_recv[s], line)
        put(mix_send, s, centred)
        start(remote(mix_send.at[s], mix_recv.at[u], mix_ssem.at[s], mix_rsem.at[u], users=s))
        statistics(stat_send, s, centred, mean)
        start(remote(stat_send.at[s], stat_recv.at[u], stat_ssem.at[s], stat_rsem.at[u], users=s))

    pl.when(jnp.logical_not(u == 0))(own_slot)

    def product(o, block):
        mixed = (mix_recv[o].astype(F32) * gate_v[block]).astype(BF16)
        part_v[m, o] = jnp.dot(mixed, wout_v[...], preferred_element_type=F32).astype(BF16)
        for d in range(1, parts):
            p = off(m, d, parts)
            start(remote(part_v.at[m, o], part_v.at[m, o], part_ssem.at[p, o], part_rsem.at[m, o], mp=p))

    product(u, own_block)
    for d in range(1, owners):
        s = targets[d]
        remote(mix_send.at[s], mix_recv.at[s], mix_ssem.at[s], mix_rsem.at[s], users=s).wait_recv()
        if d == owners - 1:
            for t in targets[1:]:
                remote(stat_send.at[t], stat_recv.at[t], stat_ssem.at[t], stat_rsem.at[t], users=t).wait_recv()
            for b in range(blocks):
                stat_v[m, b] = stat_recv[owner[b]]
            for e in range(1, parts):
                p = off(m, e, parts)
                start(remote(stat_v.at[m], stat_v.at[m], norm_ssem.at[p], norm_rsem.at[m], mp=p))
        product(s, routes[d][0])
    for d in range(1, parts):
        p = off(m, d, parts)
        remote(wsc_v.at[p], wsc_v.at[p], wsc_ssem.at[p], wsc_rsem.at[p], mp=p).wait_recv()
        remote(base_v.at[p], base_v.at[p], base_ssem.at[p], base_rsem.at[p], mp=p).wait_recv()
        remote(stat_v.at[p], stat_v.at[p], norm_ssem.at[p], norm_rsem.at[p], mp=p).wait_recv()

    def column(tiled):
        return jnp.concatenate([tiled[b][:, t : t + 1] for b in range(blocks) for t in range(tiles)], axis=0)

    stats = [[stat_v[p, b] for b in range(blocks)] for p in range(parts)]
    row_mean = [sum(stats[p][b] for p in range(parts)) / parts for b in range(blocks)]
    factor = []
    for b in range(blocks):
        spread = pltpu.roll(row_mean[b], LANES - tiles, 1) / local
        for p in range(parts):
            shift = stats[p][b] - row_mean[b]
            spread = spread + shift * shift / parts
        factor.append(lax.rsqrt(spread + EPSILON))
    factor = column(factor)
    base = jnp.zeros((rows, width), F32)
    for p in range(parts):
        shift = column([stats[p][b] - row_mean[b] for b in range(blocks)])
        base = base + shift * base_v[p].astype(F32)
    rest_v[...] = x_v[...].reshape(rows, width).astype(F32) + base * factor
    for copy in sends:
        copy.wait_send()
    for d in range(1, parts):
        p = off(m, d, parts)
        for o in targets:
            remote(part_v.at[p, o], part_v.at[p, o], part_ssem.at[p, o], part_rsem.at[p, o], mp=p).wait_recv()
    part = jnp.concatenate(
        [sum(part_v[p, owner[b]].astype(F32) for p in range(parts)) for b in range(blocks)], axis=0
    )
    shown = silu(rest_v[...] + part * factor)
    folded = jnp.zeros((rows, LANES), F32)
    for p in range(parts):
        for k in range(local // LANES):
            term = shown[:, p * local + k * LANES : p * local + (k + 1) * LANES]
            folded = folded + term * wsc_v[p, :, pl.ds(k * LANES, LANES)]
    block_rows = out_ref.shape[1]
    spot = lax.broadcasted_iota(jnp.int32, (1, block_rows), 1)
    for b in range(blocks):
        square_tile = jnp.concatenate(
            [folded[b * most : (b + 1) * most], jnp.zeros((block_rows - most, LANES), F32)], axis=0
        )
        scores = jnp.sum(square_tile.T, axis=0, keepdims=True)
        out_ref[pl.ds(b, 1), :] = jnp.where(spot < count_ref[b], scores, 0.0)


def solution(mesh):
    owners, parts = (mesh.shape[a] for a in ("users", "mp"))

    def local_fn(
        candidates,
        block_user,
        block_count,
        own_map,
        history_key_cache,
        cache_values,
        w_query_unit,
        time_bias,
        output_weight,
        w_score,
    ):
        blocks, block_rows, width = candidates.shape
        users_here, length, local = history_key_cache.shape
        heads = time_bias.shape[0]
        depth = output_weight.shape[0]
        rows = blocks * MOST
        dma = pltpu.SemaphoreType.DMA
        any_spec = pl.BlockSpec(memory_space=pl.ANY)
        return pl.pallas_call(
            functools.partial(kernel, (owners, parts)),
            out_shape=jax.ShapeDtypeStruct((blocks, block_rows), F32),
            in_specs=[any_spec] * 10,
            out_specs=pl.BlockSpec(memory_space=pltpu.VMEM),
            scratch_shapes=[
                pltpu.SMEM(block_user.shape, jnp.int32),
                pltpu.SMEM(block_count.shape, jnp.int32),
                pltpu.SMEM(own_map.shape, jnp.int32),
                pltpu.VMEM((blocks, MOST, width), BF16),
                pltpu.VMEM(w_query_unit.shape, BF16),
                pltpu.VMEM(history_key_cache.shape, BF16),
                pltpu.VMEM(cache_values.shape, BF16),
                pltpu.VMEM((depth, width), BF16),
                pltpu.VMEM((heads, length), F32),
                pltpu.VMEM((parts, 1, local), F32),
                pltpu.VMEM((blocks, MOST, local), BF16),
                pltpu.VMEM((owners, MOST, local), BF16),
                pltpu.VMEM((owners, MOST, local), BF16),
                pltpu.VMEM((owners, SUBLANES, LANES), jnp.int32),
                pltpu.VMEM((owners, SUBLANES, LANES), jnp.int32),
                pltpu.VMEM((blocks, MOST, local), F32),
                pltpu.VMEM((owners, MOST, local), BF16),
                pltpu.VMEM((owners, MOST, local), BF16),
                pltpu.VMEM((owners, SUBLANES, LANES), F32),
                pltpu.VMEM((owners, SUBLANES, LANES), F32),
                pltpu.VMEM((parts, blocks, SUBLANES, LANES), F32),
                pltpu.VMEM((parts, rows, width), BF16),
                pltpu.VMEM((parts, owners, MOST, width), BF16),
                pltpu.VMEM((rows, width), F32),
                dma((blocks + 10,)),
                dma((owners,)),
                dma((owners,)),
                dma((owners,)),
                dma((owners,)),
                dma((owners,)),
                dma((owners,)),
                dma((owners,)),
                dma((owners,)),
                dma((parts,)),
                dma((parts,)),
                dma((parts,)),
                dma((parts,)),
                dma((parts,)),
                dma((parts,)),
                dma((parts, owners)),
                dma((parts, owners)),
                pltpu.SemaphoreType.REGULAR((owners,)),
                pltpu.SemaphoreType.REGULAR((parts,)),
            ],
            compiler_params=pltpu.CompilerParams(
                collective_id=0, has_side_effects=True, vmem_limit_bytes=32 * 1024 * 1024
            ),
        )(
            *(
                pltpu.with_memory_space_constraint(a, pltpu.HBM)
                for a in (
                    block_user,
                    block_count,
                    own_map,
                    candidates,
                    history_key_cache,
                    cache_values,
                    w_query_unit,
                    time_bias,
                    output_weight,
                    w_score.reshape(1, -1),
                )
            )
        )

    return jax.shard_map(
        local_fn,
        mesh=mesh,
        in_specs=(
            P(("groups", "users", "helpers"), None, None),
            P(("groups", "users", "helpers")),
            P(("groups", "users", "helpers")),
            P("groups"),
            P(("groups", "users"), None, "mp"),
            P(("groups", "users"), None, "mp"),
            P(None, None, "mp"),
            P("mp", None),
            P("mp", None),
            P("mp"),
        ),
        out_specs=P(("groups", "users", "helpers"), None),
        check_vma=False,
    )
```

```python
import functools

import jax
import jax.numpy as jnp
from jax import lax
from jax.experimental import pallas as pl
from jax.experimental.pallas import tpu as pltpu
from jax.sharding import PartitionSpec as P

EPSILON = 1e-05
MOST = 32
LANES = 128
SUBLANES = 8
MESH = pl.DeviceIdType.MESH
F32 = jnp.float32
BF16 = jnp.bfloat16


def silu(v):
    half = 0.5 * v
    return half + half * jnp.tanh(half)


def kernel(
    sizes,
    user_hbm,
    count_hbm,
    map_hbm,
    cand_ref,
    key_ref,
    value_ref,
    wqu_ref,
    bias_ref,
    wout_ref,
    wsc_ref,
    out_ref,
    user_ref,
    count_ref,
    map_ref,
    x_v,
    wqu_v,
    key_v,
    value_v,
    wout_v,
    bias_v,
    wsc_v,
    q_v,
    q_send,
    q_recv,
    tag_send,
    tag_recv,
    gate_v,
    mix_send,
    mix_recv,
    stat_send,
    stat_recv,
    stat_v,
    base_v,
    part_v,
    rest_v,
    load_sem,
    tag_ssem,
    tag_rsem,
    q_ssem,
    q_rsem,
    mix_ssem,
    mix_rsem,
    stat_ssem,
    stat_rsem,
    wsc_ssem,
    wsc_rsem,
    norm_ssem,
    norm_rsem,
    base_ssem,
    base_rsem,
    part_ssem,
    part_rsem,
    user_ready,
    part_ready,
):
    owners, parts = sizes
    u = lax.axis_index("users")
    m = lax.axis_index("mp")
    blocks, most, width = x_v.shape
    users_here, length, local = key_v.shape
    heads = bias_v.shape[0]
    head = local // heads
    rows = blocks * most
    tiles = most // SUBLANES

    def remote(src, dst, ssem, rsem, **device):
        return pltpu.make_async_remote_copy(
            src_ref=src,
            dst_ref=dst,
            send_sem=ssem,
            recv_sem=rsem,
            device_id=device,
            device_id_type=MESH,
        )

    def off(index, step, size):
        return lax.rem(index + step, size)

    def peer(k):
        return k + (k - u + owners) // owners

    barrier = pltpu.get_barrier_semaphore()
    for o in range(owners):

        @pl.when(o > u)
        def _():
            pl.semaphore_signal(barrier, inc=1, device_id={"users": o}, device_id_type=MESH)

    for p in range(parts):

        @pl.when(p > m)
        def _():
            pl.semaphore_signal(barrier, inc=1, device_id={"mp": p}, device_id_type=MESH)


    @pl.when(u + m > 0)
    def _():
        pl.semaphore_wait(barrier, u + m)

    for o in range(owners):

        @pl.when(o < u)
        def _():
            pl.semaphore_signal(user_ready.at[u], inc=1, device_id={"users": o}, device_id_type=MESH)

    for p in range(parts):

        @pl.when(p < m)
        def _():
            pl.semaphore_signal(part_ready.at[m], inc=1, device_id={"mp": p}, device_id_type=MESH)

    def await_user(o):
        @pl.when(o > u)
        def _():
            pl.semaphore_wait(user_ready.at[o], 1)

    def await_parts():
        for p in range(parts):

            @pl.when(p > m)
            def _():
                pl.semaphore_wait(part_ready.at[p], 1)

    n = blocks
    scalars = [
        pltpu.make_async_copy(src, dst, load_sem.at[n + 7 + i])
        for i, (src, dst) in enumerate(
            ((user_hbm, user_ref), (map_hbm, map_ref), (count_hbm, count_ref))
        )
    ]
    loads = [pltpu.make_async_copy(cand_ref.at[b, pl.ds(0, most)], x_v.at[b], load_sem.at[b]) for b in range(blocks)]
    load_q = pltpu.make_async_copy(wqu_ref.at[0], wqu_v.at[0], load_sem.at[n])
    load_g = pltpu.make_async_copy(wqu_ref.at[1], wqu_v.at[1], load_sem.at[n + 1])
    load_k = pltpu.make_async_copy(key_ref, key_v, load_sem.at[n + 2])
    load_v = pltpu.make_async_copy(value_ref, value_v, load_sem.at[n + 3])
    load_w = pltpu.make_async_copy(wout_ref, wout_v, load_sem.at[n + 4])
    load_b = pltpu.make_async_copy(bias_ref, bias_v, load_sem.at[n + 5])
    load_s = pltpu.make_async_copy(wsc_ref, wsc_v.at[m], load_sem.at[n + 6])
    for load in scalars + loads + [load_q, load_s, load_b, load_g, load_w, load_k, load_v]:
        load.start()
    for load in scalars:
        load.wait()

    place = [map_ref[user_ref[b]] for b in range(blocks)]
    owner = [p // users_here for p in place]
    row = [p - o * users_here for p, o in zip(place, owner)]

    def routed(o):
        block, line = jnp.int32(0), jnp.int32(0)
        for b in range(blocks):
            hit = owner[b] == o
            block = jnp.where(hit, b, block)
            line = jnp.where(hit, row[b], line)
        return block, line

    targets = [u] + [peer(k) for k in range(owners - 1)]
    routes = [routed(o) for o in targets]
    for o, (block, line) in zip(targets, routes):
        tag_send[o] = jnp.full(tag_send.shape[1:], line, jnp.int32)

    for load in loads:
        load.wait()
    load_q.wait()
    x = x_v[...].reshape(rows, width)
    query = silu(jnp.dot(x, wqu_v[0], preferred_element_type=F32)).astype(BF16)
    q_v[...] = query.reshape(blocks, most, local)
    for d in range(1, owners):
        q_send[targets[d]] = q_v[routes[d][0]]

    sends = []

    def start(copy):
        copy.start()
        sends.append(copy)

    def send_query(d):
        o = targets[d]
        await_user(o)
        start(remote(tag_send.at[o], tag_recv.at[u], tag_ssem.at[o], tag_rsem.at[u], users=o))
        start(remote(q_send.at[o], q_recv.at[u], q_ssem.at[o], q_rsem.at[u], users=o))

    for d in range(1, owners - 1):
        send_query(d)
    load_g.wait()
    gate = silu(jnp.dot(x, wqu_v[1], preferred_element_type=F32))
    gate_v[...] = gate.reshape(blocks, most, local)
    load_w.wait()
    base_v[m] = jnp.dot(gate.astype(BF16), wout_v[...], preferred_element_type=F32).astype(BF16)
    for d in range(owners - 1, owners):
        send_query(d)
    load_s.wait()
    await_parts()
    for d in range(1, parts):
        p = off(m, d, parts)
        start(remote(wsc_v.at[m], wsc_v.at[m], wsc_ssem.at[p], wsc_rsem.at[m], mp=p))
        start(remote(base_v.at[m], base_v.at[m], base_ssem.at[p], base_rsem.at[m], mp=p))

    load_b.wait()
    load_k.wait()
    load_v.wait()
    scale = head ** (-0.5)
    lane = lax.broadcasted_iota(jnp.int32, (SUBLANES, LANES), 1)

    def attend(query, line):
        found = []
        for h in range(heads):
            cols = pl.ds(h * head, head)
            logits = lax.dot_general(
                query[:, h * head : (h + 1) * head], key_v[line, :, cols], (((1,), (1,)), ((), ())), preferred_element_type=F32
            )
            half = logits * (0.5 * scale) + 0.5 * bias_v[pl.ds(h, 1), :]
            found.append((half + half * jnp.tanh(half)).astype(BF16))
        mixed = jnp.dot(jnp.concatenate(found, axis=0), value_v[line], preferred_element_type=F32)
        found = [mixed[h * most : (h + 1) * most, h * head : (h + 1) * head] for h in range(heads)]
        mean = jnp.sum(sum(found), axis=1, keepdims=True) / local
        return [f - mean for f in found], mean

    def put(ref, index, centred):
        for h in range(heads):
            ref[index, :, pl.ds(h * head, head)] = centred[h].astype(BF16)

    def statistics(ref, index, centred, mean):
        square = jnp.sum(sum(f * f for f in centred), axis=1, keepdims=True)
        stat = jnp.zeros((SUBLANES, LANES), F32)
        for t in range(tiles):
            part = slice(t * SUBLANES, (t + 1) * SUBLANES)
            stat = jnp.where(lane == t, mean[part], stat)
            stat = jnp.where(lane == tiles + t, square[part], stat)
        ref[index] = stat

    own_block, own_line = routes[0]

    def own_slot():
        centred, mean = attend(q_v[own_block], own_line)
        put(mix_recv, u, centred)
        statistics(stat_recv, u, centred, mean)

    pl.when(u == 0)(own_slot)
    for d in range(1, owners):
        s = targets[d]
        remote(tag_send.at[s], tag_recv.at[s], tag_ssem.at[s], tag_rsem.at[s], users=s).wait_recv()
        line = tag_recv[s, 0, 0]
        remote(q_send.at[s], q_recv.at[s], q_ssem.at[s], q_rsem.at[s], users=s).wait_recv()
        centred, mean = attend(q_recv[s], line)
        put(mix_send, s, centred)
        start(remote(mix_send.at[s], mix_recv.at[u], mix_ssem.at[s], mix_rsem.at[u], users=s))
        statistics(stat_send, s, centred, mean)
        start(remote(stat_send.at[s], stat_recv.at[u], stat_ssem.at[s], stat_rsem.at[u], users=s))

    pl.when(jnp.logical_not(u == 0))(own_slot)

    def product(o, block):
        mixed = (mix_recv[o].astype(F32) * gate_v[block]).astype(BF16)
        part_v[m, o] = jnp.dot(mixed, wout_v[...], preferred_element_type=F32).astype(BF16)
        for d in range(1, parts):
            p = off(m, d, parts)
            start(remote(part_v.at[m, o], part_v.at[m, o], part_ssem.at[p, o], part_rsem.at[m, o], mp=p))

    product(u, own_block)
    for d in range(1, owners):
        s = targets[d]
        remote(mix_send.at[s], mix_recv.at[s], mix_ssem.at[s], mix_rsem.at[s], users=s).wait_recv()
        if d == owners - 1:
            for t in targets[1:]:
                remote(stat_send.at[t], stat_recv.at[t], stat_ssem.at[t], stat_rsem.at[t], users=t).wait_recv()
            for b in range(blocks):
                stat_v[m, b] = stat_recv[owner[b]]
            for e in range(1, parts):
                p = off(m, e, parts)
                start(remote(stat_v.at[m], stat_v.at[m], norm_ssem.at[p], norm_rsem.at[m], mp=p))
        product(s, routes[d][0])
    for d in range(1, parts):
        p = off(m, d, parts)
        remote(wsc_v.at[p], wsc_v.at[p], wsc_ssem.at[p], wsc_rsem.at[p], mp=p).wait_recv()
        remote(base_v.at[p], base_v.at[p], base_ssem.at[p], base_rsem.at[p], mp=p).wait_recv()
        remote(stat_v.at[p], stat_v.at[p], norm_ssem.at[p], norm_rsem.at[p], mp=p).wait_recv()

    def column(tiled):
        return jnp.concatenate([tiled[b][:, t : t + 1] for b in range(blocks) for t in range(tiles)], axis=0)

    stats = [[stat_v[p, b] for b in range(blocks)] for p in range(parts)]
    row_mean = [sum(stats[p][b] for p in range(parts)) / parts for b in range(blocks)]
    factor = []
    for b in range(blocks):
        spread = pltpu.roll(row_mean[b], LANES - tiles, 1) / local
        for p in range(parts):
            shift = stats[p][b] - row_mean[b]
            spread = spread + shift * shift / parts
        factor.append(lax.rsqrt(spread + EPSILON))
    factor = column(factor)
    base = jnp.zeros((rows, width), F32)
    for p in range(parts):
        shift = column([stats[p][b] - row_mean[b] for b in range(blocks)])
        base = base + shift * base_v[p].astype(F32)
    rest_v[...] = x_v[...].reshape(rows, width).astype(F32) + base * factor
    for copy in sends[: 1 - parts]:
        copy.wait_send()
    for d in range(1, parts):
        p = off(m, d, parts)
        for o in targets:
            remote(part_v.at[p, o], part_v.at[p, o], part_ssem.at[p, o], part_rsem.at[p, o], mp=p).wait_recv()
    part = jnp.concatenate(
        [sum(part_v[p, owner[b]].astype(F32) for p in range(parts)) for b in range(blocks)], axis=0
    )
    shown = silu(rest_v[...] + part * factor)
    folded = jnp.zeros((rows, LANES), F32)
    for p in range(parts):
        for k in range(local // LANES):
            term = shown[:, p * local + k * LANES : p * local + (k + 1) * LANES]
            folded = folded + term * wsc_v[p, :, pl.ds(k * LANES, LANES)]
    block_rows = out_ref.shape[1]
    spot = lax.broadcasted_iota(jnp.int32, (1, block_rows), 1)
    for b in range(blocks):
        square_tile = jnp.concatenate(
            [folded[b * most : (b + 1) * most], jnp.zeros((block_rows - most, LANES), F32)], axis=0
        )
        scores = jnp.sum(square_tile.T, axis=0, keepdims=True)
        out_ref[pl.ds(b, 1), :] = jnp.where(spot < count_ref[b], scores, 0.0)


    for copy in sends[1 - parts :]:
        copy.wait_send()


def solution(mesh):
    owners, parts = (mesh.shape[a] for a in ("users", "mp"))

    def local_fn(
        candidates,
        block_user,
        block_count,
        own_map,
        history_key_cache,
        cache_values,
        w_query_unit,
        time_bias,
        output_weight,
        w_score,
    ):
        blocks, block_rows, width = candidates.shape
        users_here, length, local = history_key_cache.shape
        heads = time_bias.shape[0]
        depth = output_weight.shape[0]
        rows = blocks * MOST
        dma = pltpu.SemaphoreType.DMA
        any_spec = pl.BlockSpec(memory_space=pl.ANY)
        return pl.pallas_call(
            functools.partial(kernel, (owners, parts)),
            out_shape=jax.ShapeDtypeStruct((blocks, block_rows), F32),
            in_specs=[any_spec] * 10,
            out_specs=pl.BlockSpec(memory_space=pltpu.VMEM),
            scratch_shapes=[
                pltpu.SMEM(block_user.shape, jnp.int32),
                pltpu.SMEM(block_count.shape, jnp.int32),
                pltpu.SMEM(own_map.shape, jnp.int32),
                pltpu.VMEM((blocks, MOST, width), BF16),
                pltpu.VMEM(w_query_unit.shape, BF16),
                pltpu.VMEM(history_key_cache.shape, BF16),
                pltpu.VMEM(cache_values.shape, BF16),
                pltpu.VMEM((depth, width), BF16),
                pltpu.VMEM((heads, length), F32),
                pltpu.VMEM((parts, 1, local), F32),
                pltpu.VMEM((blocks, MOST, local), BF16),
                pltpu.VMEM((owners, MOST, local), BF16),
                pltpu.VMEM((owners, MOST, local), BF16),
                pltpu.VMEM((owners, SUBLANES, LANES), jnp.int32),
                pltpu.VMEM((owners, SUBLANES, LANES), jnp.int32),
                pltpu.VMEM((blocks, MOST, local), F32),
                pltpu.VMEM((owners, MOST, local), BF16),
                pltpu.VMEM((owners, MOST, local), BF16),
                pltpu.VMEM((owners, SUBLANES, LANES), F32),
                pltpu.VMEM((owners, SUBLANES, LANES), F32),
                pltpu.VMEM((parts, blocks, SUBLANES, LANES), F32),
                pltpu.VMEM((parts, rows, width), BF16),
                pltpu.VMEM((parts, owners, MOST, width), BF16),
                pltpu.VMEM((rows, width), F32),
                dma((blocks + 10,)),
                dma((owners,)),
                dma((owners,)),
                dma((owners,)),
                dma((owners,)),
                dma((owners,)),
                dma((owners,)),
                dma((owners,)),
                dma((owners,)),
                dma((parts,)),
                dma((parts,)),
                dma((parts,)),
                dma((parts,)),
                dma((parts,)),
                dma((parts,)),
                dma((parts, owners)),
                dma((parts, owners)),
                pltpu.SemaphoreType.REGULAR((owners,)),
                pltpu.SemaphoreType.REGULAR((parts,)),
            ],
            compiler_params=pltpu.CompilerParams(
                collective_id=0, has_side_effects=True, vmem_limit_bytes=32 * 1024 * 1024
            ),
        )(
            *(
                pltpu.with_memory_space_constraint(a, pltpu.HBM)
                for a in (
                    block_user,
                    block_count,
                    own_map,
                    candidates,
                    history_key_cache,
                    cache_values,
                    w_query_unit,
                    time_bias,
                    output_weight,
                    w_score.reshape(1, -1),
                )
            )
        )

    return jax.shard_map(
        local_fn,
        mesh=mesh,
        in_specs=(
            P(("groups", "users", "helpers"), None, None),
            P(("groups", "users", "helpers")),
            P(("groups", "users", "helpers")),
            P("groups"),
            P(("groups", "users"), None, "mp"),
            P(("groups", "users"), None, "mp"),
            P(None, None, "mp"),
            P("mp", None),
            P("mp", None),
            P("mp"),
        ),
        out_specs=P(("groups", "users", "helpers"), None),
        check_vma=False,
    )
```

```python
import functools

import jax
import jax.numpy as jnp
from jax import lax
from jax.experimental import pallas as pl
from jax.experimental.pallas import tpu as pltpu
from jax.sharding import PartitionSpec as P

EPSILON = 1e-05
MOST = 32
LANES = 128
SUBLANES = 8
MESH = pl.DeviceIdType.MESH
F32 = jnp.float32
BF16 = jnp.bfloat16


def silu(v):
    half = 0.5 * v
    return half + half * jnp.tanh(half)


def kernel(
    sizes,
    user_hbm,
    count_hbm,
    map_hbm,
    cand_ref,
    key_ref,
    value_ref,
    wqu_ref,
    bias_ref,
    wout_ref,
    wsc_ref,
    out_ref,
    user_ref,
    count_ref,
    map_ref,
    x_v,
    wqu_v,
    key_v,
    value_v,
    wout_v,
    bias_v,
    wsc_v,
    q_v,
    q_send,
    q_recv,
    tag_send,
    tag_recv,
    gate_v,
    mix_send,
    mix_recv,
    stat_send,
    stat_recv,
    stat_v,
    base_v,
    part_v,
    rest_v,
    load_sem,
    tag_ssem,
    tag_rsem,
    q_ssem,
    q_rsem,
    mix_ssem,
    mix_rsem,
    stat_ssem,
    stat_rsem,
    wsc_ssem,
    wsc_rsem,
    norm_ssem,
    norm_rsem,
    base_ssem,
    base_rsem,
    part_ssem,
    part_rsem,
    user_ready,
    part_ready,
):
    owners, parts = sizes
    u = lax.axis_index("users")
    m = lax.axis_index("mp")
    blocks, most, width = x_v.shape
    users_here, length, local = key_v.shape
    heads = bias_v.shape[0]
    head = local // heads
    rows = blocks * most
    tiles = most // SUBLANES

    def remote(src, dst, ssem, rsem, **device):
        return pltpu.make_async_remote_copy(
            src_ref=src,
            dst_ref=dst,
            send_sem=ssem,
            recv_sem=rsem,
            device_id=device,
            device_id_type=MESH,
        )

    def off(index, step, size):
        return lax.rem(index + step, size)

    def peer(k):
        return k + (k - u + owners) // owners

    barrier = pltpu.get_barrier_semaphore()
    for o in range(owners):

        @pl.when(o > u)
        def _():
            pl.semaphore_signal(barrier, inc=1, device_id={"users": o}, device_id_type=MESH)

    for p in range(parts):

        @pl.when(p > m)
        def _():
            pl.semaphore_signal(barrier, inc=1, device_id={"mp": p}, device_id_type=MESH)


    @pl.when(u + m > 0)
    def _():
        pl.semaphore_wait(barrier, u + m)

    for o in range(owners):

        @pl.when(o < u)
        def _():
            pl.semaphore_signal(user_ready.at[u], inc=1, device_id={"users": o}, device_id_type=MESH)

    for p in range(parts):

        @pl.when(p < m)
        def _():
            pl.semaphore_signal(part_ready.at[m], inc=1, device_id={"mp": p}, device_id_type=MESH)

    def await_user(o):
        @pl.when(o > u)
        def _():
            pl.semaphore_wait(user_ready.at[o], 1)

    def await_parts():
        for p in range(parts):

            @pl.when(p > m)
            def _():
                pl.semaphore_wait(part_ready.at[p], 1)

    n = blocks
    scalars = [
        pltpu.make_async_copy(src, dst, load_sem.at[n + 7 + i])
        for i, (src, dst) in enumerate(
            ((user_hbm, user_ref), (map_hbm, map_ref), (count_hbm, count_ref))
        )
    ]
    loads = [pltpu.make_async_copy(cand_ref.at[b, pl.ds(0, most)], x_v.at[b], load_sem.at[b]) for b in range(blocks)]
    load_q = pltpu.make_async_copy(wqu_ref.at[0], wqu_v.at[0], load_sem.at[n])
    load_g = pltpu.make_async_copy(wqu_ref.at[1], wqu_v.at[1], load_sem.at[n + 1])
    load_k = pltpu.make_async_copy(key_ref, key_v, load_sem.at[n + 2])
    load_v = pltpu.make_async_copy(value_ref, value_v, load_sem.at[n + 3])
    load_w = pltpu.make_async_copy(wout_ref, wout_v, load_sem.at[n + 4])
    load_b = pltpu.make_async_copy(bias_ref, bias_v, load_sem.at[n + 5])
    load_s = pltpu.make_async_copy(wsc_ref, wsc_v.at[m], load_sem.at[n + 6])
    for load in scalars + loads + [load_q, load_s, load_b, load_g, load_w, load_k, load_v]:
        load.start()
    for load in scalars:
        load.wait()

    place = [map_ref[user_ref[b]] for b in range(blocks)]
    owner = [p // users_here for p in place]
    row = [p - o * users_here for p, o in zip(place, owner)]

    def routed(o):
        block, line = jnp.int32(0), jnp.int32(0)
        for b in range(blocks):
            hit = owner[b] == o
            block = jnp.where(hit, b, block)
            line = jnp.where(hit, row[b], line)
        return block, line

    targets = [u] + [peer(k) for k in range(owners - 1)]
    routes = [routed(o) for o in targets]
    for o, (block, line) in zip(targets, routes):
        tag_send[o] = jnp.full(tag_send.shape[1:], line, jnp.int32)

    for load in loads:
        load.wait()
    load_q.wait()
    x = x_v[...].reshape(rows, width)
    query = silu(jnp.dot(x, wqu_v[0], preferred_element_type=F32)).astype(BF16)
    q_v[...] = query.reshape(blocks, most, local)
    for d in range(1, owners):
        q_send[targets[d]] = q_v[routes[d][0]]

    sends = []

    def start(copy):
        copy.start()
        sends.append(copy)

    def send_query(d):
        o = targets[d]
        await_user(o)
        start(remote(tag_send.at[o], tag_recv.at[u], tag_ssem.at[o], tag_rsem.at[u], users=o))
        start(remote(q_send.at[o], q_recv.at[u], q_ssem.at[o], q_rsem.at[u], users=o))

    for d in range(1, owners - 1):
        send_query(d)
    load_g.wait()
    gate = silu(jnp.dot(x, wqu_v[1], preferred_element_type=F32))
    gate_v[...] = gate.reshape(blocks, most, local)
    load_w.wait()
    base_v[m] = jnp.dot(gate.astype(BF16), wout_v[...], preferred_element_type=F32).astype(BF16)
    for d in range(owners - 1, owners):
        send_query(d)
    load_s.wait()
    await_parts()
    for d in range(1, parts):
        p = off(m, d, parts)
        start(remote(wsc_v.at[m], wsc_v.at[m], wsc_ssem.at[p], wsc_rsem.at[m], mp=p))
        start(remote(base_v.at[m], base_v.at[m], base_ssem.at[p], base_rsem.at[m], mp=p))

    load_b.wait()
    load_k.wait()
    load_v.wait()
    scale = head ** (-0.5)
    lane = lax.broadcasted_iota(jnp.int32, (SUBLANES, LANES), 1)

    def attend(query, line):
        found = []
        for h in range(heads):
            cols = pl.ds(h * head, head)
            logits = lax.dot_general(
                query[:, h * head : (h + 1) * head], key_v[line, :, cols], (((1,), (1,)), ((), ())), preferred_element_type=F32
            )
            half = logits * (0.5 * scale) + 0.5 * bias_v[pl.ds(h, 1), :]
            found.append((half + half * jnp.tanh(half)).astype(BF16))
        mixed = jnp.dot(jnp.concatenate(found, axis=0), value_v[line], preferred_element_type=F32)
        found = [mixed[h * most : (h + 1) * most, h * head : (h + 1) * head] for h in range(heads)]
        mean = jnp.sum(sum(found), axis=1, keepdims=True) / local
        return [f - mean for f in found], mean

    def put(ref, index, centred):
        for h in range(heads):
            ref[index, :, pl.ds(h * head, head)] = centred[h].astype(BF16)

    def statistics(ref, index, centred, mean):
        square = jnp.sum(sum(f * f for f in centred), axis=1, keepdims=True)
        stat = jnp.zeros((SUBLANES, LANES), F32)
        for t in range(tiles):
            part = slice(t * SUBLANES, (t + 1) * SUBLANES)
            stat = jnp.where(lane == t, mean[part], stat)
            stat = jnp.where(lane == tiles + t, square[part], stat)
        ref[index] = stat

    def exchange(o):
        return [
            remote(part_v.at[m, o], part_v.at[m, o], part_ssem.at[p, o], part_rsem.at[m, o], mp=p)
            for p in (off(m, d, parts) for d in range(1, parts))
        ]

    def product(o, block):
        mixed = (mix_recv[o].astype(F32) * gate_v[block]).astype(BF16)
        part_v[m, o] = jnp.dot(mixed, wout_v[...], preferred_element_type=F32).astype(BF16)
        for copy in exchange(o):
            copy.start()

    own_block, own_line = routes[0]

    def own_slot():
        centred, mean = attend(q_v[own_block], own_line)
        put(mix_recv, u, centred)
        statistics(stat_recv, u, centred, mean)
        product(u, own_block)

    pl.when(u == 0)(own_slot)
    for d in range(1, owners):
        s = targets[d]
        remote(tag_send.at[s], tag_recv.at[s], tag_ssem.at[s], tag_rsem.at[s], users=s).wait_recv()
        line = tag_recv[s, 0, 0]
        remote(q_send.at[s], q_recv.at[s], q_ssem.at[s], q_rsem.at[s], users=s).wait_recv()
        centred, mean = attend(q_recv[s], line)
        put(mix_send, s, centred)
        start(remote(mix_send.at[s], mix_recv.at[u], mix_ssem.at[s], mix_rsem.at[u], users=s))
        statistics(stat_send, s, centred, mean)
        start(remote(stat_send.at[s], stat_recv.at[u], stat_ssem.at[s], stat_rsem.at[u], users=s))

    pl.when(jnp.logical_not(u == 0))(own_slot)

    sends.extend(exchange(u))
    for d in range(1, owners):
        s = targets[d]
        remote(mix_send.at[s], mix_recv.at[s], mix_ssem.at[s], mix_rsem.at[s], users=s).wait_recv()
        if d == owners - 1:
            for t in targets[1:]:
                remote(stat_send.at[t], stat_recv.at[t], stat_ssem.at[t], stat_rsem.at[t], users=t).wait_recv()
            for b in range(blocks):
                stat_v[m, b] = stat_recv[owner[b]]
            for e in range(1, parts):
                p = off(m, e, parts)
                start(remote(stat_v.at[m], stat_v.at[m], norm_ssem.at[p], norm_rsem.at[m], mp=p))
        product(s, routes[d][0])
        sends.extend(exchange(s))
    for d in range(1, parts):
        p = off(m, d, parts)
        remote(wsc_v.at[p], wsc_v.at[p], wsc_ssem.at[p], wsc_rsem.at[p], mp=p).wait_recv()
        remote(base_v.at[p], base_v.at[p], base_ssem.at[p], base_rsem.at[p], mp=p).wait_recv()
        remote(stat_v.at[p], stat_v.at[p], norm_ssem.at[p], norm_rsem.at[p], mp=p).wait_recv()

    def column(tiled):
        return jnp.concatenate([tiled[b][:, t : t + 1] for b in range(blocks) for t in range(tiles)], axis=0)

    stats = [[stat_v[p, b] for b in range(blocks)] for p in range(parts)]
    row_mean = [sum(stats[p][b] for p in range(parts)) / parts for b in range(blocks)]
    factor = []
    for b in range(blocks):
        spread = pltpu.roll(row_mean[b], LANES - tiles, 1) / local
        for p in range(parts):
            shift = stats[p][b] - row_mean[b]
            spread = spread + shift * shift / parts
        factor.append(lax.rsqrt(spread + EPSILON))
    factor = column(factor)
    base = jnp.zeros((rows, width), F32)
    for p in range(parts):
        shift = column([stats[p][b] - row_mean[b] for b in range(blocks)])
        base = base + shift * base_v[p].astype(F32)
    rest_v[...] = x_v[...].reshape(rows, width).astype(F32) + base * factor
    for copy in sends[: 1 - parts]:
        copy.wait_send()
    for d in range(1, parts):
        p = off(m, d, parts)
        for o in targets:
            remote(part_v.at[p, o], part_v.at[p, o], part_ssem.at[p, o], part_rsem.at[p, o], mp=p).wait_recv()
    part = jnp.concatenate(
        [sum(part_v[p, owner[b]].astype(F32) for p in range(parts)) for b in range(blocks)], axis=0
    )
    shown = silu(rest_v[...] + part * factor)
    folded = jnp.zeros((rows, LANES), F32)
    for p in range(parts):
        for k in range(local // LANES):
            term = shown[:, p * local + k * LANES : p * local + (k + 1) * LANES]
            folded = folded + term * wsc_v[p, :, pl.ds(k * LANES, LANES)]
    block_rows = out_ref.shape[1]
    spot = lax.broadcasted_iota(jnp.int32, (1, block_rows), 1)
    for b in range(blocks):
        square_tile = jnp.concatenate(
            [folded[b * most : (b + 1) * most], jnp.zeros((block_rows - most, LANES), F32)], axis=0
        )
        scores = jnp.sum(square_tile.T, axis=0, keepdims=True)
        out_ref[pl.ds(b, 1), :] = jnp.where(spot < count_ref[b], scores, 0.0)


    for copy in sends[1 - parts :]:
        copy.wait_send()


def solution(mesh):
    owners, parts = (mesh.shape[a] for a in ("users", "mp"))

    def local_fn(
        candidates,
        block_user,
        block_count,
        own_map,
        history_key_cache,
        cache_values,
        w_query_unit,
        time_bias,
        output_weight,
        w_score,
    ):
        blocks, block_rows, width = candidates.shape
        users_here, length, local = history_key_cache.shape
        heads = time_bias.shape[0]
        depth = output_weight.shape[0]
        rows = blocks * MOST
        dma = pltpu.SemaphoreType.DMA
        any_spec = pl.BlockSpec(memory_space=pl.ANY)
        return pl.pallas_call(
            functools.partial(kernel, (owners, parts)),
            out_shape=jax.ShapeDtypeStruct((blocks, block_rows), F32),
            in_specs=[any_spec] * 10,
            out_specs=pl.BlockSpec(memory_space=pltpu.VMEM),
            scratch_shapes=[
                pltpu.SMEM(block_user.shape, jnp.int32),
                pltpu.SMEM(block_count.shape, jnp.int32),
                pltpu.SMEM(own_map.shape, jnp.int32),
                pltpu.VMEM((blocks, MOST, width), BF16),
                pltpu.VMEM(w_query_unit.shape, BF16),
                pltpu.VMEM(history_key_cache.shape, BF16),
                pltpu.VMEM(cache_values.shape, BF16),
                pltpu.VMEM((depth, width), BF16),
                pltpu.VMEM((heads, length), F32),
                pltpu.VMEM((parts, 1, local), F32),
                pltpu.VMEM((blocks, MOST, local), BF16),
                pltpu.VMEM((owners, MOST, local), BF16),
                pltpu.VMEM((owners, MOST, local), BF16),
                pltpu.VMEM((owners, SUBLANES, LANES), jnp.int32),
                pltpu.VMEM((owners, SUBLANES, LANES), jnp.int32),
                pltpu.VMEM((blocks, MOST, local), F32),
                pltpu.VMEM((owners, MOST, local), BF16),
                pltpu.VMEM((owners, MOST, local), BF16),
                pltpu.VMEM((owners, SUBLANES, LANES), F32),
                pltpu.VMEM((owners, SUBLANES, LANES), F32),
                pltpu.VMEM((parts, blocks, SUBLANES, LANES), F32),
                pltpu.VMEM((parts, rows, width), BF16),
                pltpu.VMEM((parts, owners, MOST, width), BF16),
                pltpu.VMEM((rows, width), F32),
                dma((blocks + 10,)),
                dma((owners,)),
                dma((owners,)),
                dma((owners,)),
                dma((owners,)),
                dma((owners,)),
                dma((owners,)),
                dma((owners,)),
                dma((owners,)),
                dma((parts,)),
                dma((parts,)),
                dma((parts,)),
                dma((parts,)),
                dma((parts,)),
                dma((parts,)),
                dma((parts, owners)),
                dma((parts, owners)),
                pltpu.SemaphoreType.REGULAR((owners,)),
                pltpu.SemaphoreType.REGULAR((parts,)),
            ],
            compiler_params=pltpu.CompilerParams(
                collective_id=0, has_side_effects=True, vmem_limit_bytes=32 * 1024 * 1024
            ),
        )(
            *(
                pltpu.with_memory_space_constraint(a, pltpu.HBM)
                for a in (
                    block_user,
                    block_count,
                    own_map,
                    candidates,
                    history_key_cache,
                    cache_values,
                    w_query_unit,
                    time_bias,
                    output_weight,
                    w_score.reshape(1, -1),
                )
            )
        )

    return jax.shard_map(
        local_fn,
        mesh=mesh,
        in_specs=(
            P(("groups", "users", "helpers"), None, None),
            P(("groups", "users", "helpers")),
            P(("groups", "users", "helpers")),
            P("groups"),
            P(("groups", "users"), None, "mp"),
            P(("groups", "users"), None, "mp"),
            P(None, None, "mp"),
            P("mp", None),
            P("mp", None),
            P("mp"),
        ),
        out_specs=P(("groups", "users", "helpers"), None),
        check_vma=False,
    )
```
